32 devices in a mesh: seq: 4 (over y, x), fsdp: 8 (over z, core).
Axes of the slice: x: 2, y: 2, z: 4, core: 2. Of those that a mesh axis runs over, the one named last changes fastest.
Arguments:
- tokens: bfloat16 [8, 1024, 768], P('fsdp', 'seq'), may hold values from -6 to 6
- norm_gain: float32 [768], replicated, may hold values from 0.1 to 1.9
- in_weight: bfloat16 [768, 3328], P('fsdp'), may hold values from -0.21875 to 0.21875
- dt_weight: bfloat16 [768, 24], P('fsdp'), may hold values from -0.21875 to 0.21875
- conv_x_weight: float32 [4, 1536], replicated, may hold values from -3 to 3
- conv_x_bias: float32 [1536], replicated, may hold values from -0.5 to 0.5
- conv_bc_weight: float32 [4, 256], replicated, may hold values from -3 to 3
- conv_bc_bias: float32 [256], replicated, may hold values from -0.5 to 0.5
- dt_bias: float32 [24], replicated, may hold values from -7 to -3
- a_log: float32 [24], replicated, may hold values from 0 to 2.77
- d_skip: float32 [24], replicated, may hold values from 0.5 to 1.5
- gate_gain: float32 [1536], replicated, may hold values from 0.1 to 1.9
- out_weight: bfloat16 [1536, 768], P('fsdp'), may hold values from -0.15625 to 0.15625
- cotangent: bfloat16 [8, 1024, 768], P('fsdp', 'seq'), may hold values from -6 to 6
Outputs:
- result: float32 [8, 1024, 768], P('fsdp', 'seq')
- grad_tokens: float32 [8, 1024, 768], P('fsdp', 'seq')
- norm_gain_grad: float32 [768], replicated
- in_weight_grad: float32 [768, 3328], P('fsdp')
- dt_weight_grad: float32 [768, 24], P('fsdp')
- conv_x_weight_grad: float32 [4, 1536], replicated
- conv_x_bias_grad: float32 [1536], replicated
- conv_bc_weight_grad: float32 [4, 256], replicated
- conv_bc_bias_grad: float32 [256], replicated
- dt_bias_grad: float32 [24], replicated
- a_log_grad: float32 [24], replicated
- d_skip_grad: float32 [24], replicated
- gate_gain_grad: float32 [1536], replicated
- out_weight_grad: float32 [1536, 768], P('fsdp')
The draws below stay inside these ranges and needn't reach their ends.
All inputs are finite; a program needn't handle non-finite values.
Results may differ from the reference program's by a relative error of at most 0.012.
The reference program's roundings to bfloat16 on the way count: a program that leaves them out, or rounds other values in their place, can miss the bound.
Values may be sent and summed in bfloat16 or wider, within the bound.
No kernel may reach another device: no remote copies, remote signals or barrier semaphores. Data moves between devices by JAX's collectives and lax.ppermute only.
A program may use at most 192 MiB of HBM per device.

```python
import jax
import jax.numpy as jnp
from jax import lax

D = 768
HEADS = 24
STATE = 128
CONV = 4
SPAN = 256
INNER = 1536
PROJ = 3328
LENGTH = 1024
SEQS = 8


def block_levels(stream_key, dims, shards, low, high):
    loudness = 1.0
    for position, parts in shards:
        steps = jax.random.uniform(jax.random.fold_in(jax.random.fold_in(stream_key, 6), position), (parts,), jnp.float32, low / len(shards), high / len(shards))
        loudness = loudness * jnp.repeat(jnp.exp(steps), dims[position] // parts).reshape((-1,) + (1,) * (len(dims) - 1 - position))
    return loudness


def centred(own_key, dims, deviation, reach, shards=(), held_as=jnp.bfloat16):
    values = jax.random.normal(own_key, dims, jnp.float32) * deviation
    if len(shards) > 0:
        values = block_levels(own_key, dims, shards, -0.22, 0.18) * values
    return jnp.clip(values, min=-reach, max=reach).astype(held_as)


def setup_inputs(seed: int = 0) -> dict:
    splits = jax.random.split(jax.random.key(seed), 15)
    tokens = centred(splits[0], (SEQS, LENGTH, D), 1.0, 6.0, ((0, 8), (1, 4)))
    norm_gain = jnp.clip(1.0 + 0.18 * jax.random.normal(splits[1], (D,), jnp.float32), 0.1, 1.9)
    in_weight = centred(splits[2], (D, PROJ), D ** -0.5, 0.21875, ((0, 8),))
    dt_weight = centred(splits[3], (D, HEADS), D ** -0.5, 0.21875, ((0, 8),))
    conv_x_weight = centred(splits[4], (CONV, INNER), CONV ** -0.5, 3.0, (), jnp.float32)
    conv_x_bias = jnp.clip(jax.random.uniform(splits[5], (INNER,), jnp.float32, -0.5, 0.5), -0.5, 0.5)
    conv_bc_weight = centred(splits[6], (CONV, 2 * STATE), CONV ** -0.5, 3.0, (), jnp.float32)
    conv_bc_bias = jnp.clip(jax.random.uniform(splits[7], (2 * STATE,), jnp.float32, -0.5, 0.5), -0.5, 0.5)
    dt_bias = jnp.clip(jax.random.uniform(splits[8], (HEADS,), jnp.float32, -7.0, -3.0), -7.0, -3.0)
    a_log = jnp.clip(jax.random.uniform(splits[9], (HEADS,), jnp.float32, 0.0, 2.77), 0.0, 2.77)
    d_skip = jnp.clip(jax.random.uniform(splits[10], (HEADS,), jnp.float32, 0.5, 1.5), 0.5, 1.5)
    gate_gain = jnp.clip(1.0 + 0.18 * jax.random.normal(splits[11], (INNER,), jnp.float32), 0.1, 1.9)
    out_weight = centred(splits[12], (INNER, D), INNER ** -0.5, 0.15625, ((0, 8),))
    cotangent = centred(splits[13], (SEQS, LENGTH, D), 1.0, 6.0, ((0, 8), (1, 4)))
    return dict(tokens=tokens, norm_gain=norm_gain, in_weight=in_weight, dt_weight=dt_weight, conv_x_weight=conv_x_weight, conv_x_bias=conv_x_bias, conv_bc_weight=conv_bc_weight, conv_bc_bias=conv_bc_bias, dt_bias=dt_bias, a_log=a_log, d_skip=d_skip, gate_gain=gate_gain, out_weight=out_weight, cotangent=cotangent)


EPSILON = 1e-05

def pre_norm(tok_float, gain_vec):
    scale_rows = lax.rsqrt(lax.optimization_barrier(jnp.mean(tok_float * tok_float, axis=-1, keepdims=True)) + EPSILON)
    return tok_float * scale_rows * gain_vec

def gate_norm(ssm_float, gate_float, gain_vec):
    gated = ssm_float * jax.nn.silu(gate_float)
    scale_rows = lax.rsqrt(lax.optimization_barrier(jnp.mean(gated * gated, axis=-1, keepdims=True)) + EPSILON)
    return gated * scale_rows * gain_vec

def causal_conv(values, tap_weights, offset):
    tap_count = tap_weights.shape[0]
    length = values.shape[0]
    padded = jnp.pad(values, ((tap_count - 1, 0), (0, 0)))
    summed = offset[None, :] + jnp.zeros_like(values)
    for tap_index in range(tap_count):
        summed = summed + tap_weights[tap_index][None, :] * padded[tap_index:tap_index + length]
    return jax.nn.silu(summed)

def block_scan(x_heads, b_rows, c_rows, step_sizes, decay_rate, block_size):
    length, head_count, head_dim = x_heads.shape
    state_size = b_rows.shape[1]
    block_count = length // block_size
    highest = lax.Precision.HIGHEST
    x_blocks = x_heads.reshape(block_count, block_size, head_count, head_dim)
    b_blocks = b_rows.reshape(block_count, block_size, state_size)
    c_blocks = c_rows.reshape(block_count, block_size, state_size)
    d_blocks = step_sizes.reshape(block_count, block_size, head_count).transpose(0, 2, 1)
    causal = jnp.arange(block_size)[:, None] >= jnp.arange(block_size)[None, :]

    def advance(carry_state, inputs):
        x_block, b_block, c_block, d_block = inputs
        decays = jnp.cumsum(d_block * decay_rate[:, None], axis=1)
        scores = jnp.dot(c_block, b_block.T, precision=highest)
        spread = decays[:, :, None] - decays[:, None, :]
        kernel = jnp.where(causal[None], jnp.exp(jnp.where(causal[None], spread, 0.0)), 0.0)
        kernel = kernel * scores[None] * d_block[:, None, :]
        within = jnp.einsum('hts,shp->thp', kernel, x_block, precision=highest)
        carried = jnp.einsum('tn,hpn->thp', c_block, carry_state, precision=highest)
        carried = carried * jnp.exp(decays).T[:, :, None]
        last_decay = decays[:, -1]
        weights_in = jnp.exp(last_decay[:, None] - decays) * d_block
        updated = carry_state * jnp.exp(last_decay)[:, None, None]
        updated = updated + jnp.einsum('hs,shp,sn->hpn', weights_in, x_block, b_block, precision=highest)
        return (updated, within + carried)
    start_state = jnp.zeros((head_count, head_dim, state_size), jnp.float32)
    unused, outputs = lax.scan(advance, start_state, (x_blocks, b_blocks, c_blocks, d_blocks))
    return outputs.reshape(length, head_count, head_dim)

def mixer(x_input, dt_input, bc_input, conv_x_weight, conv_x_bias, conv_bc_weight, conv_bc_bias, dt_bias, a_log, d_skip):
    length, inner_width = x_input.shape
    head_count = dt_input.shape[1]
    head_dim = inner_width // head_count
    state_size = bc_input.shape[1] // 2
    x_conv = causal_conv(x_input, conv_x_weight, conv_x_bias)
    bc_conv = causal_conv(bc_input, conv_bc_weight, conv_bc_bias)
    step_sizes = jax.nn.softplus(dt_input + dt_bias[None, :])
    decay_rate = -jnp.exp(a_log)
    x_heads = x_conv.reshape(length, head_count, head_dim)
    outputs = block_scan(x_heads, bc_conv[:, :state_size], bc_conv[:, state_size:], step_sizes, decay_rate, SPAN)
    outputs = outputs + d_skip[None, :, None] * x_heads
    return outputs.reshape(length, inner_width)

def rounded(values):
    return lax.optimization_barrier(values.astype(jnp.bfloat16))

def reference(tokens, norm_gain, in_weight, dt_weight, conv_x_weight, conv_x_bias, conv_bc_weight, conv_bc_bias, dt_bias, a_log, d_skip, gate_gain, out_weight, cotangent):
    small_params = (conv_x_weight, conv_x_bias, conv_bc_weight, conv_bc_bias, dt_bias, a_log, d_skip)

    def one_sequence(sums, inputs):
        tok_rows, cot_rows = inputs
        tok_float = tok_rows.astype(jnp.float32)
        normed_float, pre_back = jax.vjp(pre_norm, tok_float, norm_gain)
        normed = normed_float.astype(jnp.bfloat16)
        projected = rounded(jnp.dot(normed, in_weight, preferred_element_type=jnp.float32))
        dt_input = rounded(jnp.dot(normed, dt_weight, preferred_element_type=jnp.float32))
        gate_input = projected[:, :INNER]
        x_input = projected[:, INNER:2 * INNER]
        bc_input = projected[:, 2 * INNER:]
        ssm_float, mixer_back = jax.vjp(mixer, x_input.astype(jnp.float32), dt_input.astype(jnp.float32), bc_input.astype(jnp.float32), *small_params)
        ssm_out = rounded(ssm_float)
        mixed_float, gate_back = jax.vjp(gate_norm, ssm_out.astype(jnp.float32), gate_input.astype(jnp.float32), gate_gain)
        mixed = mixed_float.astype(jnp.bfloat16)
        result_rows = tok_float + jnp.dot(mixed, out_weight, preferred_element_type=jnp.float32)
        grad_mixed = jnp.dot(cot_rows, out_weight.T, preferred_element_type=jnp.float32)
        grad_out_weight = jnp.dot(mixed.T, cot_rows, preferred_element_type=jnp.float32)
        grad_ssm, grad_gate, grad_gate_gain = gate_back(grad_mixed)
        mixer_grads = mixer_back(rounded(grad_ssm).astype(jnp.float32))
        grad_dt = mixer_grads[1].astype(jnp.bfloat16)
        grad_proj = jnp.concatenate([grad_gate.astype(jnp.bfloat16), mixer_grads[0].astype(jnp.bfloat16), mixer_grads[2].astype(jnp.bfloat16)], axis=1)
        grad_normed = jnp.dot(grad_proj, in_weight.T, preferred_element_type=jnp.float32)
        grad_normed = grad_normed + jnp.dot(grad_dt, dt_weight.T, preferred_element_type=jnp.float32)
        grad_in_weight = jnp.dot(normed.T, grad_proj, preferred_element_type=jnp.float32)
        grad_dt_weight = jnp.dot(normed.T, grad_dt, preferred_element_type=jnp.float32)
        grad_tok, grad_norm_gain = pre_back(grad_normed)
        grad_rows = cot_rows.astype(jnp.float32) + grad_tok
        terms = (grad_norm_gain, grad_in_weight, grad_dt_weight) + tuple(mixer_grads[3:]) + (grad_gate_gain, grad_out_weight)
        new_sums = tuple((jnp.add(older, newer) for older, newer in zip(sums, terms)))
        return (new_sums, (result_rows, grad_rows))
    shapes = (norm_gain, in_weight, dt_weight) + small_params + (gate_gain, out_weight)
    start_sums = tuple((jnp.zeros(weight_array.shape, jnp.float32) for weight_array in shapes))
    sums, outputs = lax.scan(one_sequence, start_sums, (tokens, cotangent))
    result, grad_tokens = outputs
    norm_gain_grad, in_weight_grad, dt_weight_grad, conv_x_weight_grad, conv_x_bias_grad, conv_bc_weight_grad, conv_bc_bias_grad, dt_bias_grad, a_log_grad, d_skip_grad, gate_gain_grad, out_weight_grad = sums
    return (result, grad_tokens, norm_gain_grad, in_weight_grad, dt_weight_grad, conv_x_weight_grad, conv_x_bias_grad, conv_bc_weight_grad, conv_bc_bias_grad, dt_bias_grad, a_log_grad, d_skip_grad, gate_gain_grad, out_weight_grad)
```

```python
import functools

import jax
import jax.numpy as jnp
from jax import lax
from jax.experimental import pallas as pl
from jax.experimental.pallas import tpu as pltpu
from jax.sharding import PartitionSpec as P

EPSILON = 1e-05
LANES = 128
CHUNK = 128
PAD = 8
F32 = jnp.float32
BF16 = jnp.bfloat16
VMEM_LIMIT = 60 * 1024 * 1024


def mm(left, right, dims):
    return lax.dot_general(left, right, (dims, ((), ())), preferred_element_type=F32)


def mm_nn(left, right):
    return mm(left, right, ((1,), (0,)))


def mm_nt(left, right):
    return mm(left, right, ((1,), (1,)))


def mm_tn(left, right):
    return mm(left, right, ((0,), (0,)))


def mm_exact(left, right):
    return jnp.dot(left, right, precision=lax.Precision.HIGHEST, preferred_element_type=F32)


def iota(shape, axis):
    return lax.broadcasted_iota(jnp.int32, shape, axis)


def spread_heads(cols, head_count, head_dim):
    rows = cols.shape[0]
    per_tile = LANES // head_dim
    lane = iota((rows, LANES), 1)
    tiles = []
    for tile in range(head_count // per_tile):
        value = jnp.broadcast_to(cols[:, tile * per_tile : tile * per_tile + 1], (rows, LANES))
        for extra in range(1, per_tile):
            head = tile * per_tile + extra
            other = jnp.broadcast_to(cols[:, head : head + 1], (rows, LANES))
            value = jnp.where(lane >= extra * head_dim, other, value)
        tiles.append(value)
    return jnp.concatenate(tiles, axis=1)


def split_heads(tile, head_dim):
    lane = iota(tile.shape, 1)
    zero = jnp.zeros_like(tile)
    return jnp.concatenate(
        [
            jnp.where((lane >= part * head_dim) & (lane < (part + 1) * head_dim), tile, zero)
            for part in range(LANES // head_dim)
        ],
        axis=0,
    )


def conv_pre(padded_rows, taps):
    count = 4
    rows = padded_rows.shape[0] - PAD
    total = jnp.broadcast_to(taps[count : count + 1], (rows, padded_rows.shape[1]))
    for tap in range(count):
        start = PAD - (count - 1) + tap
        total = total + taps[tap : tap + 1] * padded_rows[start : start + rows]
    return total


def sigmoid(value):
    return 1.0 / (1.0 + jnp.exp(-value))


def softplus(value):
    return jnp.maximum(value, 0.0) + jnp.log1p(jnp.exp(-jnp.abs(value)))


def decay_terms(dt_rows, heads, tril):
    raw = dt_rows + heads[0:1]
    step = softplus(raw)
    decay = mm_exact(tril, step * heads[1:2])
    return raw, step, decay


def proj_columns(proj_ref, width, bc_width):
    return (
        proj_ref.at[:, width : 2 * width],
        proj_ref.at[:, 2 * width : 2 * width + bc_width],
        proj_ref.at[:, 2 * width + bc_width :],
    )


def forward_kernel(
    head_dim, proj_ref, xt_ref, bt_ref, heads_ref, y_ref, save_ref, xpad, bpad, state
):
    length, width = y_ref.shape
    x_ref, bc_ref, dt_ref = proj_columns(proj_ref, width, bt_ref.shape[1])
    head_count = width // head_dim
    per_tile = LANES // head_dim
    xpad[0:PAD] = jnp.zeros((PAD, width), F32)
    bpad[0:PAD] = jnp.zeros((PAD, bc_ref.shape[1]), F32)
    xpad[PAD:] = x_ref[...].astype(F32)
    bpad[PAD:] = bc_ref[...].astype(F32)
    state[...] = jnp.zeros_like(state)
    row = iota((CHUNK, CHUNK), 0)
    col = iota((CHUNK, CHUNK), 1)
    causal = row >= col
    tril = causal.astype(F32)
    state_size = bc_ref.shape[1] // 2

    def chunk_step(chunk, unused):
        start = pl.multiple_of(chunk * CHUNK, CHUNK)
        u_x = conv_pre(xpad[pl.ds(start, CHUNK + PAD), :], xt_ref[...])
        x = u_x * sigmoid(u_x)
        u_b = conv_pre(bpad[pl.ds(start, CHUNK + PAD), :], bt_ref[...])
        bc = (u_b * sigmoid(u_b)).astype(BF16)
        b, c = bc[:, :state_size], bc[:, state_size:]
        raw, step, decay = decay_terms(
            dt_ref[pl.ds(start, CHUNK), :].astype(F32), heads_ref[...], tril
        )
        decay_t = jnp.transpose(decay)
        step_t = jnp.transpose(step)
        scores = mm_nt(c, b)
        xb = x.astype(BF16)
        within = []
        for tile in range(width // LANES):
            mats = []
            for part in range(per_tile):
                head = tile * per_tile + part
                gap = decay[:, head : head + 1] - decay_t[head : head + 1, :]
                fade = jnp.exp(jnp.where(causal, gap, -1e30))
                mats.append((fade * scores * step_t[head : head + 1, :]).astype(BF16))
            within.append(
                mm_nn(
                    jnp.concatenate(mats, axis=1),
                    split_heads(xb[:, tile * LANES : (tile + 1) * LANES], head_dim),
                )
            )
        within = jnp.concatenate(within, axis=1)
        old = state[...]
        old_b = old.astype(BF16)
        save_ref[chunk] = old_b
        grown = spread_heads(jnp.exp(decay), head_count, head_dim)
        carried = mm_nn(c, old_b) * grown
        last = decay[CHUNK - 1 : CHUNK]
        weight = spread_heads(jnp.exp(last - decay) * step, head_count, head_dim)
        state[...] = old * spread_heads(jnp.exp(last), head_count, head_dim) + mm_tn(
            b, (weight * x).astype(BF16)
        )
        y_ref[pl.ds(start, CHUNK), :] = (within + carried + xt_ref[5:6] * x).astype(BF16)
        return unused

    lax.fori_loop(0, length // CHUNK, chunk_step, 0)


def backward_kernel(
    head_dim,
    proj_ref,
    gy_ref,
    save_ref,
    xt_ref,
    bt_ref,
    heads_ref,
    grad_ref,
    small_x_ref,
    small_b_ref,
    small_h_ref,
    xpad,
    bpad,
    dstate,
    next_x,
    next_b,
):
    length, width = gy_ref.shape
    bc_width = bt_ref.shape[1]
    x_ref, bc_ref, dt_ref = proj_columns(proj_ref, width, bc_width)
    state_size = bc_width // 2
    head_count = width // head_dim
    per_tile = LANES // head_dim
    chunks = length // CHUNK
    xpad[0:PAD] = jnp.zeros((PAD, width), F32)
    bpad[0:PAD] = jnp.zeros((PAD, bc_width), F32)
    xpad[PAD:] = x_ref[...].astype(F32)
    bpad[PAD:] = bc_ref[...].astype(F32)
    dstate[...] = jnp.zeros_like(dstate)
    next_x[...] = jnp.zeros_like(next_x)
    next_b[...] = jnp.zeros_like(next_b)
    small_x_ref[...] = jnp.zeros_like(small_x_ref)
    small_b_ref[...] = jnp.zeros_like(small_b_ref)
    small_h_ref[...] = jnp.zeros_like(small_h_ref)
    row = iota((CHUNK, CHUNK), 0)
    col = iota((CHUNK, CHUNK), 1)
    causal = row >= col
    tril = causal.astype(F32)
    triu = (row <= col).astype(F32)
    strict = (row > col).astype(F32)
    lane = iota((CHUNK, LANES), 1)
    gather_heads = (
        iota((width, LANES), 0) // head_dim == iota((width, LANES), 1)
    ).astype(F32)

    def conv_back(grad_out, pre, padded_rows, taps, following, small_ref):
        gate = sigmoid(pre)
        grad_pre = grad_out * (gate * (1.0 + pre * (1.0 - gate)))
        extended = jnp.concatenate([grad_pre, following[...]], axis=0)
        following[...] = grad_pre[:PAD]
        total = jnp.zeros_like(grad_pre)
        sums = []
        for tap in range(4):
            total = total + taps[tap : tap + 1] * extended[3 - tap : 3 - tap + CHUNK]
            begin = PAD - 3 + tap
            sums.append(
                jnp.sum(grad_pre * padded_rows[begin : begin + CHUNK], axis=0, keepdims=True)
            )
        sums.append(jnp.sum(grad_pre, axis=0, keepdims=True))
        small_ref[0:5] = small_ref[0:5] + jnp.concatenate(sums, axis=0)
        return total

    def chunk_step(index, unused):
        chunk = chunks - 1 - index
        start = pl.multiple_of(chunk * CHUNK, CHUNK)
        x_rows = xpad[pl.ds(start, CHUNK + PAD), :]
        b_rows = bpad[pl.ds(start, CHUNK + PAD), :]
        u_x = conv_pre(x_rows, xt_ref[...])
        x = u_x * sigmoid(u_x)
        u_b = conv_pre(b_rows, bt_ref[...])
        bc = (u_b * sigmoid(u_b)).astype(BF16)
        b, c = bc[:, :state_size], bc[:, state_size:]
        raw, step, decay = decay_terms(
            dt_ref[pl.ds(start, CHUNK), :].astype(F32), heads_ref[...], tril
        )
        rate = heads_ref[1:2]
        decay_t = jnp.transpose(decay)
        step_t = jnp.transpose(step)
        scores = mm_nt(c, b)
        xb = x.astype(BF16)
        gy_b = gy_ref[pl.ds(start, CHUNK), :]
        gy = gy_b.astype(F32)
        old_b = save_ref[chunk]
        dnew = dstate[...]
        dnew_b = dnew.astype(BF16)
        last = decay[CHUNK - 1 : CHUNK]

        dscores = jnp.zeros((CHUNK, CHUNK), F32)
        row_sums = jnp.zeros((CHUNK, LANES), F32)
        col_sums = []
        within = []
        for tile in range(width // LANES):
            lanes = slice(tile * LANES, (tile + 1) * LANES)
            outer = mm_nt(gy_b[:, lanes], split_heads(xb[:, lanes], head_dim))
            mats = []
            for part in range(per_tile):
                head = tile * per_tile + part
                gap = decay[:, head : head + 1] - decay_t[head : head + 1, :]
                fade = jnp.exp(jnp.where(causal, gap, -1e30))
                plain = fade * scores
                mats.append(plain.astype(BF16))
                grad = outer[:, part * CHUNK : (part + 1) * CHUNK]
                scaled = grad * step_t[head : head + 1, :]
                dscores = dscores + scaled * fade
                col_sums.append(jnp.sum(grad * plain, axis=0, keepdims=True))
                rows = jnp.sum(scaled * plain, axis=1, keepdims=True)
                row_sums = row_sums + jnp.where(lane == head, rows, 0.0)
            within.append(
                mm_tn(jnp.concatenate(mats, axis=0), split_heads(gy_b[:, lanes], head_dim))
            )
        within = jnp.concatenate(within, axis=1)
        col_sums.append(jnp.zeros((LANES - head_count, CHUNK), F32))
        col_sums = jnp.transpose(jnp.concatenate(col_sums, axis=0))

        grown_gy = spread_heads(jnp.exp(decay), head_count, head_dim) * gy
        grown_gy_b = grown_gy.astype(BF16)
        remain = jnp.exp(last - decay)
        from_state = spread_heads(remain, head_count, head_dim) * mm_nn(b, dnew_b)
        carried_dot = mm_exact(grown_gy * mm_nn(c, old_b), gather_heads)
        state_dot = mm_exact(x * from_state, gather_heads)
        step_wide = spread_heads(step, head_count, head_dim)
        weight = spread_heads(remain * step, head_count, head_dim)
        dscores_b = dscores.astype(BF16)
        dc = mm_nn(dscores_b, b) + mm_nt(grown_gy_b, old_b)
        db = mm_tn(dscores_b, c) + mm_nt((weight * x).astype(BF16), dnew_b)
        last_wide = spread_heads(jnp.exp(last), head_count, head_dim)
        overlap = jnp.sum(old_b.astype(F32) * dnew, axis=0, keepdims=True) * last_wide
        dlast = mm_exact(jnp.broadcast_to(overlap, (PAD, width)), gather_heads)[0:1]
        dstate[...] = dnew * last_wide + mm_tn(c, grown_gy_b)

        direct = col_sums + state_dot
        ddecay = row_sums + carried_dot - step * col_sums
        da = mm_exact(triu, ddecay) + mm_exact(strict, step * state_dot) + dlast
        dstep = direct + da * rate
        ddt = dstep * sigmoid(raw)
        small_h_ref[0:1] = small_h_ref[0:1] + jnp.sum(ddt, axis=0, keepdims=True)
        small_h_ref[1:2] = small_h_ref[1:2] + jnp.sum(da * step, axis=0, keepdims=True) * rate

        dx = step_wide * (within + from_state) + xt_ref[5:6] * gy
        small_x_ref[5:6] = small_x_ref[5:6] + jnp.sum(gy * x, axis=0, keepdims=True)
        dx_in = conv_back(dx, u_x, x_rows, xt_ref[...], next_x, small_x_ref)
        dbc = jnp.concatenate([db, dc], axis=1)
        dbc_in = conv_back(dbc, u_b, b_rows, bt_ref[...], next_b, small_b_ref)
        grad_ref[pl.ds(start, CHUNK), :] = jnp.concatenate([dx_in, dbc_in, ddt], axis=1).astype(
            BF16
        )
        return unused

    lax.fori_loop(0, chunks, chunk_step, 0)
    small_h_ref[2:3] = mm_exact(
        jnp.broadcast_to(small_x_ref[5:6], (PAD, width)), gather_heads
    )[0:1]


def scan_forward(head_dim, proj, x_taps, bc_taps, heads):
    length = proj.shape[0]
    width, bc_width = x_taps.shape[1], bc_taps.shape[1]
    state_size = bc_width // 2
    chunks = length // CHUNK
    return pl.pallas_call(
        functools.partial(forward_kernel, head_dim),
        out_shape=(
            jax.ShapeDtypeStruct((length, width), BF16),
            jax.ShapeDtypeStruct((chunks, state_size, width), BF16),
        ),
        scratch_shapes=[
            pltpu.VMEM((length + PAD, width), F32),
            pltpu.VMEM((length + PAD, bc_width), F32),
            pltpu.VMEM((state_size, width), F32),
        ],
        compiler_params=pltpu.CompilerParams(vmem_limit_bytes=VMEM_LIMIT),
        cost_estimate=pl.CostEstimate(
            flops=8 * length * width * CHUNK, bytes_accessed=8 * length * width, transcendentals=0
        ),
        name="scan_forward",
    )(proj, x_taps, bc_taps, heads)


def scan_backward(head_dim, proj, gy, saved, x_taps, bc_taps, heads):
    length, width = gy.shape
    bc_width = bc_taps.shape[1]
    state_size = bc_width // 2
    return pl.pallas_call(
        functools.partial(backward_kernel, head_dim),
        out_shape=(
            jax.ShapeDtypeStruct((length, width + bc_width + LANES), BF16),
            jax.ShapeDtypeStruct((PAD, width), F32),
            jax.ShapeDtypeStruct((PAD, bc_width), F32),
            jax.ShapeDtypeStruct((PAD, LANES), F32),
        ),
        scratch_shapes=[
            pltpu.VMEM((length + PAD, width), F32),
            pltpu.VMEM((length + PAD, bc_width), F32),
            pltpu.VMEM((state_size, width), F32),
            pltpu.VMEM((PAD, width), F32),
            pltpu.VMEM((PAD, bc_width), F32),
        ],
        compiler_params=pltpu.CompilerParams(vmem_limit_bytes=VMEM_LIMIT),
        cost_estimate=pl.CostEstimate(
            flops=24 * length * width * CHUNK, bytes_accessed=16 * length * width, transcendentals=0
        ),
        name="scan_backward",
    )(proj, gy, saved, x_taps, bc_taps, heads)


def put(buffer, value, index, axis=0):
    return lax.dynamic_update_index_in_dim(buffer, value, index, axis)


def take(array, index, axis=0):
    return lax.dynamic_index_in_dim(array, index, axis, keepdims=False)


class Ring:
    def __init__(self):
        self.seq = lax.axis_size("seq")
        self.fsdp = lax.axis_size("fsdp")
        self.line = self.fsdp // 2
        self.s = lax.axis_index("seq")
        f = lax.axis_index("fsdp")
        self.p, self.j = f // 2, f % 2

    def from_seq(self, value, k):
        n = self.seq
        return lax.ppermute(value, "seq", [((i + k) % n, i) for i in range(n)])

    def from_line(self, value, k):
        n = self.line
        pairs = [(((i + k) % n) * 2 + c, i * 2 + c) for i in range(n) for c in range(2)]
        return lax.ppermute(value, "fsdp", pairs)

    def from_sibling(self, value):
        return lax.ppermute(value, "fsdp", [(i ^ 1, i) for i in range(self.fsdp)])

    def gather_seq(self, value):
        whole = jnp.zeros((self.seq,) + value.shape, value.dtype)
        for k in range(self.seq):
            part = value if k == 0 else self.from_seq(value, k)
            whole = put(whole, part, (self.s + k) % self.seq)
        return whole

    def gather_line(self, value):
        whole = jnp.zeros((self.line,) + value.shape, value.dtype)
        for k in range(self.line):
            part = value if k == 0 else self.from_line(value, k)
            whole = put(whole, part, (self.p + k) % self.line)
        return whole

    def join_sibling(self, mine):
        other = self.from_sibling(mine)
        whole = jnp.zeros((mine.shape[0], 2) + mine.shape[1:], mine.dtype)
        whole = put(whole, mine, self.j, 1)
        return put(whole, other, 1 - self.j, 1)

    def sum_seq(self, blocks):
        total = take(blocks, self.s).astype(F32)
        for k in range(1, self.seq):
            total = total + self.from_seq(
                take(blocks, (self.s - k) % self.seq), k
            ).astype(F32)
        return total

    def sum_fsdp(self, blocks, extra=None):
        pairs = blocks.reshape((self.line, 2) + blocks.shape[1:])
        mine = take(pairs, self.j, 1).astype(F32)
        other = take(pairs, 1 - self.j, 1).astype(BF16)
        if extra is None:
            mine = mine + self.from_sibling(other).astype(F32)
        else:
            rows = other.shape[0] * other.shape[1]
            sent = jnp.concatenate([other.reshape((rows,) + other.shape[2:]), halves(extra)], axis=0)
            got = self.from_sibling(sent)
            mine = mine + got[:rows].reshape(other.shape).astype(F32)
            extra = extra + whole_of(got[rows:])
        total = take(mine, self.p)
        extra_total = extra
        for k in range(1, self.line):
            sent = take(mine, (self.p - k) % self.line).astype(BF16)
            if extra is None:
                total = total + self.from_line(sent, k).astype(F32)
            else:
                rows = sent.shape[0]
                got = self.from_line(jnp.concatenate([sent, halves(extra)], axis=0), k)
                total = total + got[:rows].astype(F32)
                extra_total = extra_total + whole_of(got[rows:])
        return total, extra_total


def halves(value):
    high = lax.reduce_precision(value, 8, 7)
    return jnp.concatenate([high.astype(BF16), (value - high).astype(BF16)], axis=0)


def whole_of(pair):
    rows = pair.shape[0] // 2
    return pair[:rows].astype(F32) + pair[rows:].astype(F32)


def local(
    tokens,
    norm_gain,
    in_weight,
    dt_weight,
    conv_x_weight,
    conv_x_bias,
    conv_bc_weight,
    conv_bc_bias,
    dt_bias,
    a_log,
    d_skip,
    gate_gain,
    out_weight,
    cotangent,
):
    ring = Ring()
    s, seq, fsdp = ring.s, ring.seq, ring.fsdp
    tok_rows, cot_rows = tokens[0], cotangent[0]
    rows_here, model = tok_rows.shape
    length = rows_here * seq
    inner = gate_gain.shape[0]
    width = inner // seq
    all_heads = dt_bias.shape[0]
    head_dim = inner // all_heads
    heads_here = all_heads // seq
    bc_width = conv_bc_weight.shape[1]
    shard = in_weight.shape[0]
    wide = -(-width // LANES) * LANES

    def columns(array, start, size):
        return lax.dynamic_slice_in_dim(array, start, size, 1)

    def pad_lanes(array, value=0.0, size=LANES):
        return jnp.pad(array, ((0, 0), (0, size - array.shape[1])), constant_values=value)

    x_taps = columns(
        jnp.concatenate(
            [
                conv_x_weight,
                conv_x_bias[None],
                jnp.repeat(d_skip, head_dim)[None],
                gate_gain[None],
                jnp.zeros((1, inner), F32),
            ],
            axis=0,
        ),
        s * width,
        width,
    )
    x_taps = pad_lanes(x_taps, size=wide)
    gain = x_taps[6:7]
    bc_taps = jnp.concatenate(
        [conv_bc_weight, conv_bc_bias[None], jnp.zeros((3, bc_width), F32)], axis=0
    )
    bias_here = columns(dt_bias[None], s * heads_here, heads_here)
    rate_here = -jnp.exp(columns(a_log[None], s * heads_here, heads_here))
    heads = jnp.concatenate(
        [pad_lanes(bias_here, -100.0), pad_lanes(rate_here), jnp.zeros((6, LANES), F32)], axis=0
    )

    own_weight = jnp.concatenate(
        [
            pad_lanes(columns(in_weight, s * width, width), size=wide),
            pad_lanes(columns(in_weight, inner + s * width, width), size=wide),
            in_weight[:, 2 * inner :],
            pad_lanes(columns(dt_weight, s * heads_here, heads_here)),
        ],
        axis=1,
    )
    tok_full = ring.gather_seq(tok_rows).reshape(length, model)
    weight = ring.join_sibling(ring.gather_line(own_weight)).reshape(model, -1)
    cot_full = ring.gather_seq(cot_rows).reshape(length, model)
    out_line = ring.gather_line(out_weight)
    out_rows = ring.line // seq
    out_here = lax.dynamic_slice_in_dim(out_line, s * out_rows, out_rows, 0)
    out_here = ring.join_sibling(out_here).reshape(width, model)
    out_here = jnp.pad(out_here, ((0, wide - width), (0, 0)))

    def rms(rows):
        return lax.rsqrt(jnp.mean(rows * rows, axis=-1, keepdims=True) + EPSILON)

    tok_wide = tok_full.astype(F32)
    scaled = tok_wide * rms(tok_wide)
    normed = (scaled * norm_gain).astype(BF16)
    projected = mm_nn(normed, weight).astype(BF16)
    ssm_out, saved = scan_forward(head_dim, projected, x_taps, bc_taps, heads)
    grad_mixed = mm_nt(cot_full, out_here)
    gate = projected[:, :wide].astype(F32)
    ssm = ssm_out.astype(F32)
    opened = jax.nn.sigmoid(gate)
    silu = gate * opened
    gated = ssm * silu
    gained = grad_mixed * gain
    stats = jnp.stack([jnp.sum(gated * gated, axis=1), jnp.sum(gated * gained, axis=1)])
    stats = stats + sum(ring.from_seq(stats, k) for k in range(1, seq))
    scale = lax.rsqrt(stats[0] / inner + EPSILON)[:, None]
    pull = (scale * scale * scale) * (stats[1][:, None] / inner)
    mixed_plain = gated * scale
    mixed = (mixed_plain * gain).astype(BF16)
    grad_gated = scale * gained - gated * pull
    grad_ssm = (grad_gated * silu).astype(BF16)
    grad_gate = (grad_gated * ssm * (opened * (1.0 + gate * (1.0 - opened)))).astype(BF16)
    gate_gain_part = jnp.sum(grad_mixed * mixed_plain, axis=0)

    out_part = mm_nn(mixed, out_here).astype(BF16).reshape(seq, rows_here, model)
    result = tok_rows.astype(F32) + ring.sum_seq(out_part)

    gate_weight_part = mm_tn(normed, grad_gate)[:, :width].reshape(fsdp, shard, width)
    out_weight_part = mm_tn(mixed, cot_full)[:width].reshape(fsdp, width // fsdp, model)
    early = jnp.concatenate(
        [gate_weight_part]
        + [out_weight_part[:, :, c : c + width] for c in range(0, model, width)],
        axis=1,
    )
    early, unused = ring.sum_fsdp(early)
    total = seq * fsdp
    out_block = lax.ppermute(
        early[shard:].astype(BF16),
        ("seq", "fsdp"),
        [(k, (k % seq) * fsdp + k // seq) for k in range(total)],
    )
    early = ring.gather_seq(jnp.concatenate([early[:shard].astype(BF16), out_block], axis=0))
    gate_weight_grad = early[:, :shard]
    out_weight_grad = early[:, shard:].reshape(seq, model // width, width // fsdp, width)
    out_weight_grad = out_weight_grad.transpose(0, 2, 1, 3).reshape(-1, model).astype(F32)

    grad_cols, small_x, small_bc, small_heads = scan_backward(
        head_dim, projected, grad_ssm, saved, x_taps, bc_taps, heads
    )
    gn_part = mm_nt(grad_gate, weight[:, :wide]) + mm_nt(grad_cols, weight[:, wide:])
    norm_gain_part = jnp.sum(gn_part * scaled, axis=0)
    grad_normed = ring.sum_seq(gn_part.astype(BF16).reshape(seq, rows_here, model))
    late_part = mm_tn(normed, grad_cols).reshape(fsdp, shard, -1)
    late_width = late_part.shape[2]

    pieces = [
        norm_gain_part,
        gate_gain_part[:width],
        small_x[:5, :width].reshape(-1),
        small_bc[:5].reshape(-1),
        small_heads[:3, :heads_here].reshape(-1),
    ]
    sizes = [piece.shape[0] for piece in pieces]
    flat = jnp.concatenate(pieces)
    small_rows = -(-flat.shape[0] // (8 * late_width)) * 8
    flat = jnp.pad(flat, (0, small_rows * late_width - flat.shape[0]))
    late, small = ring.sum_fsdp(late_part, flat.reshape(small_rows, late_width))
    late = ring.gather_seq(jnp.concatenate([late.astype(BF16), halves(small)], axis=0))
    small = (
        late[:, shard : shard + small_rows].astype(F32) + late[:, shard + small_rows :].astype(F32)
    ).reshape(seq, -1)
    parts = []
    at = 0
    for size in sizes:
        parts.append(small[:, at : at + size])
        at += size
    norm_gain_grad = parts[0].sum(0)
    gate_gain_grad = parts[1].reshape(-1)
    conv_x = parts[2].reshape(seq, 5, width).transpose(1, 0, 2).reshape(5, inner)
    conv_bc = parts[3].sum(0).reshape(5, bc_width)
    head_grads = parts[4].reshape(seq, 3, heads_here).transpose(1, 0, 2).reshape(3, all_heads)

    late = late[:, :shard].astype(F32)
    in_weight_grad = jnp.concatenate(
        [
            gate_weight_grad.astype(F32).transpose(1, 0, 2).reshape(shard, inner),
            late[:, :, :width].transpose(1, 0, 2).reshape(shard, inner),
            late[:, :, wide : wide + bc_width].sum(0),
        ],
        axis=1,
    )
    dt_at = wide + bc_width
    dt_weight_grad = late[:, :, dt_at : dt_at + heads_here].transpose(1, 0, 2)
    dt_weight_grad = dt_weight_grad.reshape(shard, all_heads)

    tok_wide = tok_rows.astype(F32)
    scale = rms(tok_wide)
    gained = grad_normed * norm_gain
    grad_tok = scale * gained - tok_wide * (
        scale * scale * scale * jnp.mean(gained * tok_wide, axis=-1, keepdims=True)
    )
    grad_tokens = cot_rows.astype(F32) + grad_tok
    return (
        result[None],
        grad_tokens[None],
        norm_gain_grad,
        in_weight_grad,
        dt_weight_grad,
        conv_x[:4],
        conv_x[4],
        conv_bc[:4],
        conv_bc[4],
        head_grads[0],
        head_grads[1],
        head_grads[2],
        gate_gain_grad,
        out_weight_grad,
    )


def solution(mesh):
    placed = (
        P("fsdp", "seq", None),
        P(),
        P("fsdp", None),
        P("fsdp", None),
        P(),
        P(),
        P(),
        P(),
        P(),
        P(),
        P(),
        P(),
        P("fsdp", None),
        P("fsdp", "seq", None),
    )
    return jax.shard_map(
        local,
        mesh=mesh,
        in_specs=placed,
        out_specs=(
            P("fsdp", "seq", None),
            P("fsdp", "seq", None),
            P(),
            P("fsdp", None),
            P("fsdp", None),
            P(),
            P(),
            P(),
            P(),
            P(),
            P(),
            P(),
            P(),
            P("fsdp", None),
        ),
        check_vma=False,
    )
```

```python
import functools

import jax
import jax.numpy as jnp
from jax import lax
from jax.experimental import pallas as pl
from jax.experimental.pallas import tpu as pltpu
from jax.sharding import PartitionSpec as P

EPSILON = 1e-05
LANES = 128
CHUNK = 128
PAD = 8
F32 = jnp.float32
BF16 = jnp.bfloat16
VMEM_LIMIT = 60 * 1024 * 1024


def mm(left, right, dims):
    return lax.dot_general(left, right, (dims, ((), ())), preferred_element_type=F32)


def mm_nn(left, right):
    return mm(left, right, ((1,), (0,)))


def mm_nt(left, right):
    return mm(left, right, ((1,), (1,)))


def mm_tn(left, right):
    return mm(left, right, ((0,), (0,)))


def mm_exact(left, right):
    return jnp.dot(left, right, precision=lax.Precision.HIGHEST, preferred_element_type=F32)


def iota(shape, axis):
    return lax.broadcasted_iota(jnp.int32, shape, axis)


def spread_heads(cols, head_count, head_dim):
    rows = cols.shape[0]
    per_tile = LANES // head_dim
    lane = iota((rows, LANES), 1)
    tiles = []
    for tile in range(head_count // per_tile):
        value = jnp.broadcast_to(cols[:, tile * per_tile : tile * per_tile + 1], (rows, LANES))
        for extra in range(1, per_tile):
            head = tile * per_tile + extra
            other = jnp.broadcast_to(cols[:, head : head + 1], (rows, LANES))
            value = jnp.where(lane >= extra * head_dim, other, value)
        tiles.append(value)
    return jnp.concatenate(tiles, axis=1)


def split_heads(tile, head_dim):
    lane = iota(tile.shape, 1)
    zero = jnp.zeros_like(tile)
    return jnp.concatenate(
        [
            jnp.where((lane >= part * head_dim) & (lane < (part + 1) * head_dim), tile, zero)
            for part in range(LANES // head_dim)
        ],
        axis=0,
    )


def conv_pre(padded_rows, taps):
    count = 4
    rows = padded_rows.shape[0] - PAD
    total = jnp.broadcast_to(taps[count : count + 1], (rows, padded_rows.shape[1]))
    for tap in range(count):
        start = PAD - (count - 1) + tap
        total = total + taps[tap : tap + 1] * padded_rows[start : start + rows]
    return total


def sigmoid(value):
    return 1.0 / (1.0 + jnp.exp(-value))


def softplus(value):
    return jnp.maximum(value, 0.0) + jnp.log1p(jnp.exp(-jnp.abs(value)))


def decay_terms(dt_rows, heads, tril):
    raw = dt_rows + heads[0:1]
    step = softplus(raw)
    decay = mm_exact(tril, step * heads[1:2])
    return raw, step, decay


def at_rows(index, rows):
    return pl.ds(pl.multiple_of(index * rows, rows), rows)


def forward_kernel(head_dim, dims, idx_ref, *refs):
    seq, line, parts = dims
    toks, refs = refs[:seq], refs[seq:]
    pieces, refs = refs[:parts], refs[parts:]
    gain_ref, xt_ref, bt_ref, heads_ref, proj_ref, y_ref, save_ref, weight_ref, normed_ref = refs[:9]
    xpad, bpad, state = refs[9:]
    length, width = y_ref.shape
    bc_width = bt_ref.shape[1]
    state_size = bc_width // 2
    head_count = width // head_dim
    per_tile = LANES // head_dim
    s, p, j = idx_ref[0], idx_ref[1], idx_ref[2]
    if parts == 1:
        weight_ref[...] = pieces[0][...]
    else:
        shard = pieces[0].shape[0]
        for k in range(line):
            at = lax.rem(p + k, line) * 2
            weight_ref[at_rows(at + j, shard), :] = pieces[k][...]
            weight_ref[at_rows(at + 1 - j, shard), :] = pieces[line + k][...]
    xpad[0:PAD] = jnp.zeros((PAD, width), F32)
    bpad[0:PAD] = jnp.zeros((PAD, bc_width), F32)
    rows_here = toks[0].shape[0]
    for k in range(seq):
        tok = toks[k][...].astype(F32)
        scale = lax.rsqrt(jnp.mean(tok * tok, axis=1, keepdims=True) + EPSILON)
        normed = (tok * scale * gain_ref[...]).astype(BF16)
        start = pl.multiple_of(lax.rem(s + k, seq) * rows_here, rows_here)
        normed_ref[pl.ds(start, rows_here), :] = normed
        proj = mm_nn(normed, weight_ref[...]).astype(BF16)
        proj_ref[pl.ds(start, rows_here), :] = proj
        padded = pl.multiple_of(start + PAD, PAD)
        xpad[pl.ds(padded, rows_here), :] = proj[:, width : 2 * width].astype(F32)
        bpad[pl.ds(padded, rows_here), :] = proj[:, 2 * width : 2 * width + bc_width].astype(F32)
    state[...] = jnp.zeros_like(state)
    row = iota((CHUNK, CHUNK), 0)
    col = iota((CHUNK, CHUNK), 1)
    causal = row >= col
    tril = causal.astype(F32)
    dt_at = 2 * width + bc_width

    def chunk_step(chunk, unused):
        start = pl.multiple_of(chunk * CHUNK, CHUNK)
        u_x = conv_pre(xpad[pl.ds(start, CHUNK + PAD), :], xt_ref[...])
        x = u_x * sigmoid(u_x)
        u_b = conv_pre(bpad[pl.ds(start, CHUNK + PAD), :], bt_ref[...])
        bc = (u_b * sigmoid(u_b)).astype(BF16)
        b, c = bc[:, :state_size], bc[:, state_size:]
        raw, step, decay = decay_terms(
            proj_ref[pl.ds(start, CHUNK), dt_at:].astype(F32), heads_ref[...], tril
        )
        decay_t = jnp.transpose(decay)
        step_t = jnp.transpose(step)
        scores = mm_nt(c, b)
        xb = x.astype(BF16)
        within = []
        for tile in range(width // LANES):
            mats = []
            for part in range(per_tile):
                head = tile * per_tile + part
                gap = decay[:, head : head + 1] - decay_t[head : head + 1, :]
                fade = jnp.exp(jnp.where(causal, gap, -1e30))
                mats.append((fade * scores * step_t[head : head + 1, :]).astype(BF16))
            within.append(
                mm_nn(
                    jnp.concatenate(mats, axis=1),
                    split_heads(xb[:, tile * LANES : (tile + 1) * LANES], head_dim),
                )
            )
        within = jnp.concatenate(within, axis=1)
        old = state[...]
        old_b = old.astype(BF16)
        save_ref[chunk] = old_b
        grown = spread_heads(jnp.exp(decay), head_count, head_dim)
        carried = mm_nn(c, old_b) * grown
        last = decay[CHUNK - 1 : CHUNK]
        weight = spread_heads(jnp.exp(last - decay) * step, head_count, head_dim)
        state[...] = old * spread_heads(jnp.exp(last), head_count, head_dim) + mm_tn(
            b, (weight * x).astype(BF16)
        )
        y_ref[pl.ds(start, CHUNK), :] = (within + carried + xt_ref[5:6] * x).astype(BF16)
        return unused

    lax.fori_loop(0, length // CHUNK, chunk_step, 0)


def gate_terms(proj_ref, y_ref, rows, width):
    gate = proj_ref[rows, 0:width].astype(F32)
    ssm = y_ref[rows, :].astype(F32)
    opened = sigmoid(gate)
    silu = gate * opened
    return gate, ssm, opened, silu


def stats_kernel(dims, idx_ref, *refs):
    seq = dims
    cots, refs = refs[:seq], refs[seq:]
    out_ref, proj_ref, y_ref, xt_ref, gm_ref, stats_ref = refs
    width = y_ref.shape[1]
    rows_here = cots[0].shape[0]
    s = idx_ref[0]
    lane = iota((CHUNK, LANES), 1)
    for k in range(seq):
        base = lax.rem(s + k, seq) * rows_here
        grad_mixed = mm_nt(cots[k][...], out_ref[...])
        gm_ref[pl.ds(pl.multiple_of(base, rows_here), rows_here), :] = grad_mixed
        for part in range(rows_here // CHUNK):
            start = pl.multiple_of(base + part * CHUNK, CHUNK)
            gate, ssm, opened, silu = gate_terms(proj_ref, y_ref, pl.ds(start, CHUNK), width)
            gated = ssm * silu
            gained = grad_mixed[part * CHUNK : (part + 1) * CHUNK] * xt_ref[6:7]
            squares = jnp.sum(gated * gated, axis=1, keepdims=True)
            cross = jnp.sum(gated * gained, axis=1, keepdims=True)
            both = jnp.where(lane == 0, squares, jnp.where(lane == 1, cross, 0.0))
            stats_ref[:, pl.ds(start, CHUNK)] = jnp.transpose(both)[:PAD]


def result_kernel(dims, idx_ref, proj_ref, y_ref, xt_ref, out_ref, *parts):
    seq = dims
    width = y_ref.shape[1]
    rows_here = parts[0].shape[0]
    s = idx_ref[0]
    for k in range(seq):
        start = pl.multiple_of(lax.rem(s + seq - k, seq) * rows_here, rows_here)
        gate, ssm, opened, silu = gate_terms(proj_ref, y_ref, pl.ds(start, rows_here), width)
        value = (ssm * silu * xt_ref[6:7]).astype(BF16)
        parts[k][...] = mm_nn(value, out_ref[...]).astype(parts[k].dtype)


def gate_kernel(dims, idx_ref, *refs):
    seq, line, inner, packed = dims
    cots, refs = refs[:seq], refs[seq:]
    stats, refs = refs[:seq], refs[seq:]
    proj_ref, y_ref, gm_ref, xt_ref, normed_ref, gy_ref, gg_ref, gain_part_ref = refs[:8]
    refs = refs[8:]
    if packed:
        keep_ref, send_ref = refs[:2]
        mixed, gate_w, out_w = refs[2:]
    else:
        gate_w, out_w, mixed = refs
    length, width = y_ref.shape
    rows_here = cots[0].shape[0]
    model = normed_ref.shape[1]
    s, j = idx_ref[0], idx_ref[2]
    gain = xt_ref[6:7]

    def chunk_step(chunk, total):
        start = pl.multiple_of(chunk * CHUNK, CHUNK)
        both = stats[0][:, pl.ds(start, CHUNK)]
        for k in range(1, seq):
            both = both + stats[k][:, pl.ds(start, CHUNK)]
        both = jnp.transpose(jnp.concatenate([both, jnp.zeros((LANES - PAD, CHUNK), F32)], axis=0))
        scale = lax.rsqrt(both[:, 0:1] / inner + EPSILON)
        pull = scale * scale * scale * (both[:, 1:2] / inner)
        rows = pl.ds(start, CHUNK)
        gate, ssm, opened, silu = gate_terms(proj_ref, y_ref, rows, width)
        gated = ssm * silu
        grad_mixed = gm_ref[rows, :]
        plain = gated * scale
        mixed[rows, :] = (plain * gain).astype(BF16)
        grad_gated = scale * (grad_mixed * gain) - gated * pull
        gy_ref[rows, :] = (grad_gated * silu).astype(BF16)
        slope = opened * (1.0 + gate * (1.0 - opened))
        gg_ref[rows, :] = (grad_gated * ssm * slope).astype(BF16)
        return total + jnp.sum(grad_mixed * plain, axis=0, keepdims=True)

    gain_part_ref[0:1] = lax.fori_loop(0, length // CHUNK, chunk_step, jnp.zeros((1, width), F32))

    gate_w[...] = jnp.zeros_like(gate_w)
    out_w[...] = jnp.zeros_like(out_w)
    for k in range(seq):
        start = pl.multiple_of(lax.rem(s + k, seq) * rows_here, rows_here)
        rows = pl.ds(start, rows_here)
        gate_w[...] += mm_tn(normed_ref[rows, :], gg_ref[rows, :])
        out_w[...] += mm_tn(mixed[rows, :], cots[k][...])
    if packed:
        shard = model // (2 * line)
        piece = width // (2 * line)
        for p in range(line):
            for ref, parity in ((keep_ref, j), (send_ref, 1 - j)):
                at = 2 * p + parity
                ref[p, 0:shard, :] = gate_w[at_rows(at, shard), :].astype(ref.dtype)
                for c in range(model // width):
                    ref[p, shard + c * piece : shard + (c + 1) * piece, :] = out_w[
                        at_rows(at, piece), c * width : (c + 1) * width
                    ].astype(ref.dtype)


def backward_kernel(head_dim, dims, idx_ref, *refs):
    seq, line, first, final, packed = dims
    proj_ref, gy_ref, save_ref, xt_ref, bt_ref, heads_ref = refs[:6]
    refs = refs[6:]
    if not first:
        carried, refs = refs[:7], refs[7:]
    if final:
        gg_ref, weight_ref, normed_ref, gain_ref, gain_part_ref = refs[:5]
        gn_refs, refs = refs[5 : 5 + seq], refs[5 + seq :]
        if packed:
            keep_ref, send_ref, small_ref = refs[:3]
            refs = refs[3:]
        else:
            late_w, small_ref = refs[:2]
            refs = refs[2:]
        grad_ref, small_x_ref, small_b_ref, small_h_ref, dstate, next_x, next_b = refs[:7]
        refs = refs[7:]
        if packed:
            late_w, refs = refs[0], refs[1:]
        gn_scratch, xpad, bpad = refs
    else:
        grad_ref, small_x_ref, small_b_ref, small_h_ref, dstate, next_x, next_b = refs[:7]
        xpad, bpad = refs[7:]
    length, width = gy_ref.shape
    bc_width = bt_ref.shape[1]
    state_size = bc_width // 2
    head_count = width // head_dim
    per_tile = LANES // head_dim
    chunks = length // CHUNK
    half = chunks // 2
    dt_at = 2 * width + bc_width
    xpad[0:PAD] = jnp.zeros((PAD, width), F32)
    bpad[0:PAD] = jnp.zeros((PAD, bc_width), F32)
    low = 0 if final else half * CHUNK - PAD
    high = length if first else half * CHUNK
    xpad[PAD + low : PAD + high] = proj_ref[low:high, width : 2 * width].astype(F32)
    bpad[PAD + low : PAD + high] = proj_ref[low:high, 2 * width : dt_at].astype(F32)
    if first:
        for ref in (small_x_ref, small_b_ref, small_h_ref, dstate, next_x, next_b):
            ref[...] = jnp.zeros_like(ref)
    else:
        for ref, old in zip(
            (small_x_ref, small_b_ref, small_h_ref, dstate, next_x, next_b), carried[1:]
        ):
            ref[...] = old[...]
        grad_ref[half * CHUNK :, :] = carried[0][half * CHUNK :, :]
    row = iota((CHUNK, CHUNK), 0)
    col = iota((CHUNK, CHUNK), 1)
    causal = row >= col
    tril = causal.astype(F32)
    triu = (row <= col).astype(F32)
    strict = (row > col).astype(F32)
    lane = iota((CHUNK, LANES), 1)
    gather_heads = (
        iota((width, LANES), 0) // head_dim == iota((width, LANES), 1)
    ).astype(F32)

    def conv_back(grad_out, pre, padded_rows, taps, following, small_ref):
        gate = sigmoid(pre)
        grad_pre = grad_out * (gate * (1.0 + pre * (1.0 - gate)))
        extended = jnp.concatenate([grad_pre, following[...]], axis=0)
        following[...] = grad_pre[:PAD]
        total = jnp.zeros_like(grad_pre)
        sums = []
        for tap in range(4):
            total = total + taps[tap : tap + 1] * extended[3 - tap : 3 - tap + CHUNK]
            begin = PAD - 3 + tap
            sums.append(
                jnp.sum(grad_pre * padded_rows[begin : begin + CHUNK], axis=0, keepdims=True)
            )
        sums.append(jnp.sum(grad_pre, axis=0, keepdims=True))
        small_ref[0:5] = small_ref[0:5] + jnp.concatenate(sums, axis=0)
        return total

    def chunk_step(index, unused):
        chunk = (chunks if first else half) - 1 - index
        start = pl.multiple_of(chunk * CHUNK, CHUNK)
        x_rows = xpad[pl.ds(start, CHUNK + PAD), :]
        b_rows = bpad[pl.ds(start, CHUNK + PAD), :]
        u_x = conv_pre(x_rows, xt_ref[...])
        x = u_x * sigmoid(u_x)
        u_b = conv_pre(b_rows, bt_ref[...])
        bc = (u_b * sigmoid(u_b)).astype(BF16)
        b, c = bc[:, :state_size], bc[:, state_size:]
        raw, step, decay = decay_terms(
            proj_ref[pl.ds(start, CHUNK), dt_at:].astype(F32), heads_ref[...], tril
        )
        rate = heads_ref[1:2]
        decay_t = jnp.transpose(decay)
        step_t = jnp.transpose(step)
        scores = mm_nt(c, b)
        xb = x.astype(BF16)
        gy_b = gy_ref[pl.ds(start, CHUNK), :]
        gy = gy_b.astype(F32)
        old_b = save_ref[chunk]
        dnew = dstate[...]
        dnew_b = dnew.astype(BF16)
        last = decay[CHUNK - 1 : CHUNK]

        dscores = jnp.zeros((CHUNK, CHUNK), F32)
        row_sums = jnp.zeros((CHUNK, LANES), F32)
        col_sums = []
        within = []
        for tile in range(width // LANES):
            lanes = slice(tile * LANES, (tile + 1) * LANES)
            outer = mm_nt(gy_b[:, lanes], split_heads(xb[:, lanes], head_dim))
            mats = []
            for part in range(per_tile):
                head = tile * per_tile + part
                gap = decay[:, head : head + 1] - decay_t[head : head + 1, :]
                fade = jnp.exp(jnp.where(causal, gap, -1e30))
                plain = fade * scores
                mats.append(plain.astype(BF16))
                grad = outer[:, part * CHUNK : (part + 1) * CHUNK]
                scaled = grad * step_t[head : head + 1, :]
                dscores = dscores + scaled * fade
                col_sums.append(jnp.sum(grad * plain, axis=0, keepdims=True))
                rows = jnp.sum(scaled * plain, axis=1, keepdims=True)
                row_sums = row_sums + jnp.where(lane == head, rows, 0.0)
            within.append(
                mm_tn(jnp.concatenate(mats, axis=0), split_heads(gy_b[:, lanes], head_dim))
            )
        within = jnp.concatenate(within, axis=1)
        col_sums.append(jnp.zeros((LANES - head_count, CHUNK), F32))
        col_sums = jnp.transpose(jnp.concatenate(col_sums, axis=0))

        grown_gy = spread_heads(jnp.exp(decay), head_count, head_dim) * gy
        grown_gy_b = grown_gy.astype(BF16)
        remain = jnp.exp(last - decay)
        from_state = spread_heads(remain, head_count, head_dim) * mm_nn(b, dnew_b)
        carried_dot = mm_exact(grown_gy * mm_nn(c, old_b), gather_heads)
        state_dot = mm_exact(x * from_state, gather_heads)
        step_wide = spread_heads(step, head_count, head_dim)
        weight = spread_heads(remain * step, head_count, head_dim)
        dscores_b = dscores.astype(BF16)
        dc = mm_nn(dscores_b, b) + mm_nt(grown_gy_b, old_b)
        db = mm_tn(dscores_b, c) + mm_nt((weight * x).astype(BF16), dnew_b)
        last_wide = spread_heads(jnp.exp(last), head_count, head_dim)
        overlap = jnp.sum(old_b.astype(F32) * dnew, axis=0, keepdims=True) * last_wide
        dlast = mm_exact(jnp.broadcast_to(overlap, (PAD, width)), gather_heads)[0:1]
        dstate[...] = dnew * last_wide + mm_tn(c, grown_gy_b)

        direct = col_sums + state_dot
        ddecay = row_sums + carried_dot - step * col_sums
        da = mm_exact(triu, ddecay) + mm_exact(strict, step * state_dot) + dlast
        dstep = direct + da * rate
        ddt = dstep * sigmoid(raw)
        small_h_ref[0:1] = small_h_ref[0:1] + jnp.sum(ddt, axis=0, keepdims=True)
        small_h_ref[1:2] = small_h_ref[1:2] + jnp.sum(da * step, axis=0, keepdims=True) * rate

        dx = step_wide * (within + from_state) + xt_ref[5:6] * gy
        small_x_ref[5:6] = small_x_ref[5:6] + jnp.sum(gy * x, axis=0, keepdims=True)
        dx_in = conv_back(dx, u_x, x_rows, xt_ref[...], next_x, small_x_ref)
        dbc = jnp.concatenate([db, dc], axis=1)
        dbc_in = conv_back(dbc, u_b, b_rows, bt_ref[...], next_b, small_b_ref)
        grad_ref[pl.ds(start, CHUNK), :] = jnp.concatenate([dx_in, dbc_in, ddt], axis=1).astype(
            BF16
        )
        return unused

    lax.fori_loop(0, chunks - half if first else half, chunk_step, 0)
    if not final:
        return
    small_h_ref[2:3] = mm_exact(
        jnp.broadcast_to(small_x_ref[5:6], (PAD, width)), gather_heads
    )[0:1]
    s, j = idx_ref[0], idx_ref[2]
    model = normed_ref.shape[1]
    rows_here = gn_refs[0].shape[0]
    late_width = late_w.shape[1]
    gain_sum = jnp.zeros((1, model), F32)
    for k in range(seq):
        rows = pl.ds(pl.multiple_of(lax.rem(s + seq - k, seq) * rows_here, rows_here), rows_here)
        gn = mm_nt(gg_ref[rows, :], weight_ref[:, 0:width]) + mm_nt(
            grad_ref[rows, :], weight_ref[:, width:]
        )
        gn_refs[k][...] = gn.astype(gn_refs[k].dtype)
        gain_sum = gain_sum + jnp.sum(gn * normed_ref[rows, :].astype(F32), axis=0, keepdims=True)
        late = mm_tn(normed_ref[rows, :], grad_ref[rows, :])
        late_w[...] = late if k == 0 else late_w[...] + late
    gain_sum = gain_sum / gain_ref[...]
    small_ref[...] = jnp.zeros_like(small_ref)
    small_ref[0:5, 0:width] = small_x_ref[0:5]
    small_ref[0:5, width : width + bc_width] = small_b_ref[0:5]
    small_ref[0:3, width + bc_width :] = small_h_ref[0:3]
    small_ref[5:6, 0:width] = gain_part_ref[0:1]
    for c in range(0, model, late_width):
        size = min(late_width, model - c)
        at = 6 + c // late_width
        small_ref[at : at + 1, 0:size] = gain_sum[:, c : c + size]
    if packed:
        shard = model // (2 * line)
        for p in range(line):
            keep_ref[p] = late_w[at_rows(2 * p + j, shard), :]
            send_ref[p * shard : (p + 1) * shard, :] = late_w[
                at_rows(2 * p + 1 - j, shard), :
            ].astype(BF16)
        high = small_ref[...].astype(BF16)
        send_ref[line * shard : line * shard + PAD, :] = high
        send_ref[line * shard + PAD :, :] = (small_ref[...] - high.astype(F32)).astype(BF16)


VMEM_SPEC = pl.BlockSpec(memory_space=pltpu.VMEM)
SMEM_SPEC = pl.BlockSpec(memory_space=pltpu.SMEM)


def call(kernel, name, idx, arrays, outs, scratch, flops):
    bytes_moved = sum(a.size * a.dtype.itemsize for a in list(arrays) + list(outs))
    return pl.pallas_call(
        kernel,
        out_shape=tuple(outs),
        in_specs=[SMEM_SPEC] + [VMEM_SPEC] * len(arrays),
        out_specs=tuple([VMEM_SPEC] * len(outs)),
        scratch_shapes=[pltpu.VMEM(*one) for one in scratch],
        compiler_params=pltpu.CompilerParams(vmem_limit_bytes=VMEM_LIMIT),
        cost_estimate=pl.CostEstimate(
            flops=int(flops), bytes_accessed=int(bytes_moved), transcendentals=0
        ),
        name=name,
    )(idx, *arrays)


def shaped(shape, dtype):
    return jax.ShapeDtypeStruct(shape, dtype)


def put(buffer, value, index, axis=0):
    return lax.dynamic_update_index_in_dim(buffer, value, index, axis)


def take(array, index, axis=0):
    return lax.dynamic_index_in_dim(array, index, axis, keepdims=False)


class Ring:
    def __init__(self):
        self.seq = lax.axis_size("seq")
        self.fsdp = lax.axis_size("fsdp")
        self.line = self.fsdp // 2
        self.s = lax.axis_index("seq")
        f = lax.axis_index("fsdp")
        self.p, self.j = f // 2, f % 2

    def from_seq(self, value, k):
        n = self.seq
        return lax.ppermute(value, "seq", [((i + k) % n, i) for i in range(n)])

    def from_line(self, value, k):
        n = self.line
        pairs = [(((i + k) % n) * 2 + c, i * 2 + c) for i in range(n) for c in range(2)]
        return lax.ppermute(value, "fsdp", pairs)

    def from_sibling(self, value):
        return lax.ppermute(value, "fsdp", [(i ^ 1, i) for i in range(self.fsdp)])

    def parts_seq(self, value):
        return [value] + [self.from_seq(value, k) for k in range(1, self.seq)]

    def parts_line(self, value):
        return [value] + [self.from_line(value, k) for k in range(1, self.line)]

    def gather_seq(self, value):
        whole = jnp.zeros((self.seq,) + value.shape, value.dtype)
        for k in range(self.seq):
            part = value if k == 0 else self.from_seq(value, k)
            whole = put(whole, part, (self.s + k) % self.seq)
        return whole

    def gather_line(self, value):
        whole = jnp.zeros((self.line,) + value.shape, value.dtype)
        for k in range(self.line):
            part = value if k == 0 else self.from_line(value, k)
            whole = put(whole, part, (self.p + k) % self.line)
        return whole

    def join_sibling(self, mine):
        other = self.from_sibling(mine)
        whole = jnp.zeros((mine.shape[0], 2) + mine.shape[1:], mine.dtype)
        whole = put(whole, mine, self.j, 1)
        return put(whole, other, 1 - self.j, 1)

    def sum_seq(self, blocks):
        total = take(blocks, self.s).astype(F32)
        for k in range(1, self.seq):
            total = total + self.from_seq(
                take(blocks, (self.s - k) % self.seq), k
            ).astype(F32)
        return total

    def pair_split(self, blocks, extra=None):
        pairs = blocks.reshape((self.line, 2) + blocks.shape[1:])
        keep = take(pairs, self.j, 1)
        send = take(pairs, 1 - self.j, 1).astype(BF16)
        if extra is None:
            return keep, send
        send = send.reshape((-1, send.shape[2]))
        return keep, jnp.concatenate([send, halves(extra)], axis=0)

    def sum_fsdp(self, keep, send, extra=None):
        got = self.from_sibling(send)
        if extra is None:
            mine = keep + got.astype(F32)
        else:
            rows = keep.shape[0] * keep.shape[1]
            mine = keep + got[:rows].reshape(keep.shape).astype(F32)
            extra = extra + whole_of(got[rows:])
        total = take(mine, self.p)
        extra_total = extra
        for k in range(1, self.line):
            sent = take(mine, (self.p - k) % self.line).astype(BF16)
            if extra is None:
                total = total + self.from_line(sent, k).astype(F32)
            else:
                rows = sent.shape[0]
                got = self.from_line(jnp.concatenate([sent, halves(extra)], axis=0), k)
                total = total + got[:rows].astype(F32)
                extra_total = extra_total + whole_of(got[rows:])
        return total, extra_total


def halves(value):
    high = lax.reduce_precision(value, 8, 7)
    return jnp.concatenate([high.astype(BF16), (value - high).astype(BF16)], axis=0)


def whole_of(pair):
    rows = pair.shape[0] // 2
    return pair[:rows].astype(F32) + pair[rows:].astype(F32)


def local(
    tokens,
    norm_gain,
    in_weight,
    dt_weight,
    conv_x_weight,
    conv_x_bias,
    conv_bc_weight,
    conv_bc_bias,
    dt_bias,
    a_log,
    d_skip,
    gate_gain,
    out_weight,
    cotangent,
):
    ring = Ring()
    s, seq, fsdp, line = ring.s, ring.seq, ring.fsdp, ring.line
    idx = jnp.stack([ring.s, ring.p, ring.j]).astype(jnp.int32)
    tok_rows, cot_rows = tokens[0], cotangent[0]
    rows_here, model = tok_rows.shape
    length = rows_here * seq
    inner = gate_gain.shape[0]
    width = inner // seq
    all_heads = dt_bias.shape[0]
    head_dim = inner // all_heads
    heads_here = all_heads // seq
    bc_width = conv_bc_weight.shape[1]
    state_size = bc_width // 2
    shard = in_weight.shape[0]
    wide = -(-width // LANES) * LANES
    late_width = wide + bc_width + LANES
    chunks = length // CHUNK
    packed = wide == width and shard % 16 == 0 and (width // fsdp) % 16 == 0 and model % width == 0

    def columns(array, start, size):
        return lax.dynamic_slice_in_dim(array, start, size, 1)

    def pad_lanes(array, value=0.0, size=LANES):
        return jnp.pad(array, ((0, 0), (0, size - array.shape[1])), constant_values=value)

    own_weight = jnp.concatenate(
        [
            pad_lanes(columns(in_weight, s * width, width), size=wide),
            pad_lanes(columns(in_weight, inner + s * width, width), size=wide),
            in_weight[:, 2 * inner :],
            pad_lanes(columns(dt_weight, s * heads_here, heads_here)),
        ],
        axis=1,
    )
    tok_parts = ring.parts_seq(tok_rows)
    if packed:
        lane_parts = ring.parts_line(own_weight)
        pieces = lane_parts + [ring.from_sibling(part) for part in lane_parts]
    else:
        pieces = [ring.join_sibling(ring.gather_line(own_weight)).reshape(model, -1)]
    tok_parts, pieces, cot_rows, out_weight = lax.optimization_barrier(
        (tok_parts, pieces, cot_rows, out_weight)
    )
    cot_parts = ring.parts_seq(cot_rows)
    out_rows = line // seq
    out_mine = []
    for r in range(out_rows):
        place = s * out_rows + r
        value = jnp.where(ring.p == place, out_weight, jnp.zeros_like(out_weight))
        for k in range(1, line):
            pairs = []
            for one in range(seq):
                src = one * out_rows + r
                dst = (src + k) % line
                for c in range(2):
                    pairs.append((one * fsdp + 2 * src + c, one * fsdp + 2 * dst + c))
            value = value + lax.ppermute(out_weight, ("seq", "fsdp"), pairs)
        out_mine.append(value)
    out_here = ring.join_sibling(jnp.stack(out_mine)).reshape(width, model)
    out_here = jnp.pad(out_here, ((0, wide - width), (0, 0)))

    x_taps = columns(
        jnp.concatenate(
            [
                conv_x_weight,
                conv_x_bias[None],
                jnp.repeat(d_skip, head_dim)[None],
                gate_gain[None],
                jnp.zeros((1, inner), F32),
            ],
            axis=0,
        ),
        s * width,
        width,
    )
    x_taps = pad_lanes(x_taps, size=wide)
    bc_taps = jnp.concatenate(
        [conv_bc_weight, conv_bc_bias[None], jnp.zeros((3, bc_width), F32)], axis=0
    )
    bias_here = columns(dt_bias[None], s * heads_here, heads_here)
    rate_here = -jnp.exp(columns(a_log[None], s * heads_here, heads_here))
    heads = jnp.concatenate(
        [pad_lanes(bias_here, -100.0), pad_lanes(rate_here), jnp.zeros((6, LANES), F32)], axis=0
    )
    gain_row = norm_gain[None]

    pads = [((length + PAD, wide), F32), ((length + PAD, bc_width), F32)]
    projected, ssm_out, saved, weight, normed = call(
        functools.partial(forward_kernel, head_dim, (seq, line, len(pieces))),
        "project_scan",
        idx,
        tok_parts + pieces + [gain_row, x_taps, bc_taps, heads],
        [
            shaped((length, wide + late_width), BF16),
            shaped((length, wide), BF16),
            shaped((chunks, state_size, wide), BF16),
            shaped((model, wide + late_width), BF16),
            shaped((length, model), BF16),
        ],
        pads + [((state_size, wide), F32)],
        8 * length * wide * CHUNK,
    )
    grad_mixed, stats = call(
        functools.partial(stats_kernel, seq),
        "gate_stats",
        idx,
        cot_parts + [out_here, projected, ssm_out, x_taps],
        [shaped((length, wide), F32), shaped((PAD, length), F32)],
        [],
        2 * length * wide * model,
    )
    stat_parts = ring.parts_seq(stats)
    out_parts = call(
        functools.partial(result_kernel, seq),
        "out_project",
        idx,
        [projected, ssm_out, x_taps, out_here],
        [shaped((rows_here, model), F32 if k == 0 else BF16) for k in range(seq)],
        [],
        2 * length * wide * model,
    )
    out_sum = out_parts[0]
    for k in range(1, seq):
        out_sum = out_sum + ring.from_seq(out_parts[k], k).astype(F32)

    extra_rows = (width // fsdp) * (model // width)
    grid_w = ((model, wide), F32), ((wide, model), F32), ((length, wide), BF16)
    if packed:
        outs = [
            shaped((line, shard + extra_rows, width), F32),
            shaped((line, shard + extra_rows, width), BF16),
        ]
        scratch = [grid_w[2], grid_w[0], grid_w[1]]
    else:
        outs = [shaped(*grid_w[0]), shaped(*grid_w[1])]
        scratch = [grid_w[2]]
    grad_ssm, grad_gate, gain_part, one, two = call(
        functools.partial(gate_kernel, (seq, line, inner, packed)),
        "gate_backward",
        idx,
        cot_parts + stat_parts + [projected, ssm_out, grad_mixed, x_taps, normed],
        [
            shaped((length, wide), BF16),
            shaped((length, wide), BF16),
            shaped((PAD, wide), F32),
        ]
        + outs,
        scratch,
        4 * length * wide * model,
    )
    if packed:
        keep, send = one, two
    else:
        out_blocks = two[:width].reshape(fsdp, width // fsdp, model)
        keep, send = ring.pair_split(
            jnp.concatenate(
                [one[:, :width].reshape(fsdp, shard, width)]
                + [out_blocks[:, :, c : c + width] for c in range(0, model, width)],
                axis=1,
            )
        )
    early, unused = ring.sum_fsdp(keep, send)
    out_block = lax.ppermute(
        early[shard:].astype(BF16),
        ("seq", "fsdp"),
        [(k, (k % seq) * fsdp + k // seq) for k in range(seq * fsdp)],
    )
    early = ring.gather_seq(jnp.concatenate([early[:shard].astype(BF16), out_block], axis=0))
    gate_weight_grad = early[:, :shard]
    out_weight_grad = early[:, shard:].reshape(seq, model // width, width // fsdp, width)
    out_weight_grad = out_weight_grad.transpose(0, 2, 1, 3).reshape(-1, model).astype(F32)

    stats_here = lax.dynamic_slice_in_dim(sum(stat_parts)[0], s * rows_here, rows_here, 0)
    out_scale = lax.rsqrt(stats_here / inner + EPSILON)[:, None]
    result = tok_rows.astype(F32) + out_sum * out_scale

    base = [projected, grad_ssm, saved, x_taps, bc_taps, heads]
    state_outs = [
        shaped((length, late_width), BF16),
        shaped((PAD, wide), F32),
        shaped((PAD, bc_width), F32),
        shaped((PAD, LANES), F32),
        shaped((state_size, wide), F32),
        shaped((PAD, wide), F32),
        shaped((PAD, bc_width), F32),
    ]
    carried = call(
        functools.partial(backward_kernel, head_dim, (seq, line, True, False, packed)),
        "scan_back_late",
        idx,
        base,
        state_outs,
        pads,
        12 * length * wide * CHUNK,
    )
    small_shape = ((PAD, late_width), F32)
    late_shape = ((model, late_width), F32)
    if packed:
        outs = [
            shaped((line, shard, late_width), F32),
            shaped((line * shard + 2 * PAD, late_width), BF16),
            shaped(*small_shape),
        ]
        scratch = [(o.shape, o.dtype) for o in state_outs] + [late_shape]
    else:
        outs = [shaped(*late_shape), shaped(*small_shape)]
        scratch = [(o.shape, o.dtype) for o in state_outs]
    done = call(
        functools.partial(backward_kernel, head_dim, (seq, line, False, True, packed)),
        "scan_back_early",
        idx,
        base + list(carried) + [grad_gate, weight, normed, gain_row, gain_part],
        [shaped((rows_here, model), F32 if k == 0 else BF16) for k in range(seq)] + outs,
        scratch + [((PAD, LANES), F32)] + pads,
        12 * length * wide * CHUNK + 4 * length * model * late_width,
    )
    gn_parts, done = done[:seq], done[seq:]
    grad_normed = gn_parts[0]
    for k in range(1, seq):
        grad_normed = grad_normed + ring.from_seq(gn_parts[k], k).astype(F32)
    if packed:
        keep, send, small = done
    else:
        late_part, small = done
        keep, send = ring.pair_split(late_part.reshape(fsdp, shard, late_width), small)
    late, small = ring.sum_fsdp(keep, send, small)
    late = ring.gather_seq(jnp.concatenate([late.astype(BF16), halves(small)], axis=0))
    small = late[:, shard : shard + PAD].astype(F32) + late[:, shard + PAD :].astype(F32)
    head_at = wide + bc_width
    conv_x = small[:, :5, :width].transpose(1, 0, 2).reshape(5, inner)
    conv_bc = small[:, :5, wide:head_at].sum(0)
    head_grads = small[:, :3, head_at : head_at + heads_here].transpose(1, 0, 2)
    head_grads = head_grads.reshape(3, all_heads)
    gate_gain_grad = small[:, 5, :width].reshape(-1)
    norm_gain_grad = small[:, 6:].sum(0).reshape(-1)[:model]

    late = late[:, :shard].astype(F32)
    in_weight_grad = jnp.concatenate(
        [
            gate_weight_grad.astype(F32).transpose(1, 0, 2).reshape(shard, inner),
            late[:, :, :width].transpose(1, 0, 2).reshape(shard, inner),
            late[:, :, wide:head_at].sum(0),
        ],
        axis=1,
    )
    dt_weight_grad = late[:, :, head_at : head_at + heads_here].transpose(1, 0, 2)
    dt_weight_grad = dt_weight_grad.reshape(shard, all_heads)

    tok_wide = tok_rows.astype(F32)
    scale = lax.rsqrt(jnp.mean(tok_wide * tok_wide, axis=-1, keepdims=True) + EPSILON)
    gained = grad_normed * norm_gain
    grad_tok = scale * gained - tok_wide * (
        scale * scale * scale * jnp.mean(gained * tok_wide, axis=-1, keepdims=True)
    )
    grad_tokens = cot_rows.astype(F32) + grad_tok
    return (
        result[None],
        grad_tokens[None],
        norm_gain_grad,
        in_weight_grad,
        dt_weight_grad,
        conv_x[:4],
        conv_x[4],
        conv_bc[:4],
        conv_bc[4],
        head_grads[0],
        head_grads[1],
        head_grads[2],
        gate_gain_grad,
        out_weight_grad,
    )


def solution(mesh):
    placed = (
        P("fsdp", "seq", None),
        P(),
        P("fsdp", None),
        P("fsdp", None),
        P(),
        P(),
        P(),
        P(),
        P(),
        P(),
        P(),
        P(),
        P("fsdp", None),
        P("fsdp", "seq", None),
    )
    return jax.shard_map(
        local,
        mesh=mesh,
        in_specs=placed,
        out_specs=(
            P("fsdp", "seq", None),
            P("fsdp", "seq", None),
            P(),
            P("fsdp", None),
            P("fsdp", None),
            P(),
            P(),
            P(),
            P(),
            P(),
            P(),
            P(),
            P(),
            P("fsdp", None),
        ),
        check_vma=False,
    )
```

```python
import functools

import jax
import jax.numpy as jnp
from jax import lax
from jax.experimental import pallas as pl
from jax.experimental.pallas import tpu as pltpu
from jax.sharding import PartitionSpec as P

EPSILON = 1e-05
LANES = 128
CHUNK = 128
PAD = 8
F32 = jnp.float32
BF16 = jnp.bfloat16
VMEM_LIMIT = 60 * 1024 * 1024


def mm(left, right, dims):
    return lax.dot_general(left, right, (dims, ((), ())), preferred_element_type=F32)


def mm_nn(left, right):
    return mm(left, right, ((1,), (0,)))


def mm_nt(left, right):
    return mm(left, right, ((1,), (1,)))


def mm_tn(left, right):
    return mm(left, right, ((0,), (0,)))


def mm_exact(left, right):
    return jnp.dot(left, right, precision=lax.Precision.HIGHEST, preferred_element_type=F32)


def iota(shape, axis):
    return lax.broadcasted_iota(jnp.int32, shape, axis)


def spread_heads(cols, head_count, head_dim):
    rows = cols.shape[0]
    per_tile = LANES // head_dim
    lane = iota((rows, LANES), 1)
    tiles = []
    for tile in range(head_count // per_tile):
        value = jnp.broadcast_to(cols[:, tile * per_tile : tile * per_tile + 1], (rows, LANES))
        for extra in range(1, per_tile):
            head = tile * per_tile + extra
            other = jnp.broadcast_to(cols[:, head : head + 1], (rows, LANES))
            value = jnp.where(lane >= extra * head_dim, other, value)
        tiles.append(value)
    return jnp.concatenate(tiles, axis=1)


def split_heads(tile, head_dim):
    lane = iota(tile.shape, 1)
    zero = jnp.zeros_like(tile)
    return jnp.concatenate(
        [
            jnp.where((lane >= part * head_dim) & (lane < (part + 1) * head_dim), tile, zero)
            for part in range(LANES // head_dim)
        ],
        axis=0,
    )


def conv_pre(padded_rows, taps):
    count = 4
    rows = padded_rows.shape[0] - PAD
    total = jnp.broadcast_to(taps[count : count + 1], (rows, padded_rows.shape[1]))
    for tap in range(count):
        start = PAD - (count - 1) + tap
        total = total + taps[tap : tap + 1] * padded_rows[start : start + rows]
    return total


def sigmoid(value):
    return 1.0 / (1.0 + jnp.exp(-value))


def softplus(value):
    return jnp.maximum(value, 0.0) + jnp.log1p(jnp.exp(-jnp.abs(value)))


def decay_terms(dt_rows, heads, tril):
    raw = dt_rows + heads[0:1]
    step = softplus(raw)
    decay = mm_exact(tril, step * heads[1:2])
    return raw, step, decay


def at_rows(index, rows):
    return pl.ds(pl.multiple_of(index * rows, rows), rows)


def forward_kernel(head_dim, dims, idx_ref, *refs):
    seq, line, parts = dims
    toks, refs = refs[:seq], refs[seq:]
    pieces, refs = refs[:parts], refs[parts:]
    gain_ref, xt_ref, bt_ref, heads_ref, proj_ref, y_ref, save_ref, weight_ref, normed_ref = refs[:9]
    xpad, bpad, state = refs[9:]
    length, width = y_ref.shape
    bc_width = bt_ref.shape[1]
    state_size = bc_width // 2
    head_count = width // head_dim
    per_tile = LANES // head_dim
    s, p, j = idx_ref[0], idx_ref[1], idx_ref[2]
    if parts == 1:
        weight_ref[...] = pieces[0][...]
    else:
        shard = pieces[0].shape[0]
        for k in range(line):
            at = lax.rem(p + k, line) * 2
            weight_ref[at_rows(at + j, shard), :] = pieces[k][...]
            weight_ref[at_rows(at + 1 - j, shard), :] = pieces[line + k][...]
    xpad[0:PAD] = jnp.zeros((PAD, width), F32)
    bpad[0:PAD] = jnp.zeros((PAD, bc_width), F32)
    rows_here = toks[0].shape[0]
    for k in range(seq):
        tok = toks[k][...].astype(F32)
        scale = lax.rsqrt(jnp.mean(tok * tok, axis=1, keepdims=True) + EPSILON)
        normed = (tok * scale * gain_ref[...]).astype(BF16)
        start = pl.multiple_of(lax.rem(s + k, seq) * rows_here, rows_here)
        normed_ref[pl.ds(start, rows_here), :] = normed
        proj = mm_nn(normed, weight_ref[...]).astype(BF16)
        proj_ref[pl.ds(start, rows_here), :] = proj
        padded = pl.multiple_of(start + PAD, PAD)
        xpad[pl.ds(padded, rows_here), :] = proj[:, width : 2 * width].astype(F32)
        bpad[pl.ds(padded, rows_here), :] = proj[:, 2 * width : 2 * width + bc_width].astype(F32)
    state[...] = jnp.zeros_like(state)
    row = iota((CHUNK, CHUNK), 0)
    col = iota((CHUNK, CHUNK), 1)
    causal = row >= col
    tril = causal.astype(F32)
    dt_at = 2 * width + bc_width

    def chunk_step(chunk, unused):
        start = pl.multiple_of(chunk * CHUNK, CHUNK)
        u_x = conv_pre(xpad[pl.ds(start, CHUNK + PAD), :], xt_ref[...])
        x = u_x * sigmoid(u_x)
        u_b = conv_pre(bpad[pl.ds(start, CHUNK + PAD), :], bt_ref[...])
        bc = (u_b * sigmoid(u_b)).astype(BF16)
        b, c = bc[:, :state_size], bc[:, state_size:]
        raw, step, decay = decay_terms(
            proj_ref[pl.ds(start, CHUNK), dt_at:].astype(F32), heads_ref[...], tril
        )
        decay_t = jnp.transpose(decay)
        step_t = jnp.transpose(step)
        scores = mm_nt(c, b)
        xb = x.astype(BF16)
        within = []
        for tile in range(width // LANES):
            mats = []
            for part in range(per_tile):
                head = tile * per_tile + part
                gap = decay[:, head : head + 1] - decay_t[head : head + 1, :]
                fade = jnp.exp(jnp.where(causal, gap, -1e30))
                mats.append((fade * scores * step_t[head : head + 1, :]).astype(BF16))
            within.append(
                mm_nn(
                    jnp.concatenate(mats, axis=1),
                    split_heads(xb[:, tile * LANES : (tile + 1) * LANES], head_dim),
                )
            )
        within = jnp.concatenate(within, axis=1)
        old = state[...]
        old_b = old.astype(BF16)
        save_ref[chunk] = old_b
        grown = spread_heads(jnp.exp(decay), head_count, head_dim)
        carried = mm_nn(c, old_b) * grown
        last = decay[CHUNK - 1 : CHUNK]
        weight = spread_heads(jnp.exp(last - decay) * step, head_count, head_dim)
        state[...] = old * spread_heads(jnp.exp(last), head_count, head_dim) + mm_tn(
            b, (weight * x).astype(BF16)
        )
        y_ref[pl.ds(start, CHUNK), :] = (within + carried + xt_ref[5:6] * x).astype(BF16)
        return unused

    lax.fori_loop(0, length // CHUNK, chunk_step, 0)


def gate_terms(proj_ref, y_ref, rows, width):
    gate = proj_ref[rows, 0:width].astype(F32)
    ssm = y_ref[rows, :].astype(F32)
    opened = sigmoid(gate)
    silu = gate * opened
    return gate, ssm, opened, silu


def stats_kernel(dims, idx_ref, *refs):
    seq = dims
    cots, refs = refs[:seq], refs[seq:]
    out_ref, proj_ref, y_ref, xt_ref, gm_ref, stats_ref = refs
    width = y_ref.shape[1]
    rows_here = cots[0].shape[0]
    s = idx_ref[0]
    lane = iota((CHUNK, LANES), 1)
    for k in range(seq):
        base = lax.rem(s + k, seq) * rows_here
        grad_mixed = mm_nt(cots[k][...], out_ref[...])
        gm_ref[pl.ds(pl.multiple_of(base, rows_here), rows_here), :] = grad_mixed
        for part in range(rows_here // CHUNK):
            start = pl.multiple_of(base + part * CHUNK, CHUNK)
            gate, ssm, opened, silu = gate_terms(proj_ref, y_ref, pl.ds(start, CHUNK), width)
            gated = ssm * silu
            gained = grad_mixed[part * CHUNK : (part + 1) * CHUNK] * xt_ref[6:7]
            squares = jnp.sum(gated * gated, axis=1, keepdims=True)
            cross = jnp.sum(gated * gained, axis=1, keepdims=True)
            both = jnp.where(lane == 0, squares, jnp.where(lane == 1, cross, 0.0))
            stats_ref[:, pl.ds(start, CHUNK)] = jnp.transpose(both)[:PAD]


def result_kernel(dims, idx_ref, proj_ref, y_ref, xt_ref, out_ref, *parts):
    seq = dims
    width = y_ref.shape[1]
    rows_here = parts[0].shape[0]
    s = idx_ref[0]
    for k in range(seq):
        start = pl.multiple_of(lax.rem(s + seq - k, seq) * rows_here, rows_here)
        gate, ssm, opened, silu = gate_terms(proj_ref, y_ref, pl.ds(start, rows_here), width)
        value = (ssm * silu * xt_ref[6:7]).astype(BF16)
        parts[k][...] = mm_nn(value, out_ref[...]).astype(parts[k].dtype)


def gate_kernel(dims, idx_ref, *refs):
    seq, line, inner, packed = dims
    cots, refs = refs[:seq], refs[seq:]
    stats, refs = refs[:seq], refs[seq:]
    proj_ref, y_ref, gm_ref, xt_ref, normed_ref, gy_ref, gg_ref, gain_part_ref = refs[:8]
    refs = refs[8:]
    if packed:
        keep_ref, send_ref = refs[:2]
        mixed, gate_w, out_w = refs[2:]
    else:
        gate_w, out_w, mixed = refs
    length, width = y_ref.shape
    rows_here = cots[0].shape[0]
    model = normed_ref.shape[1]
    s, j = idx_ref[0], idx_ref[2]
    gain = xt_ref[6:7]

    def chunk_step(chunk, total):
        start = pl.multiple_of(chunk * CHUNK, CHUNK)
        both = stats[0][:, pl.ds(start, CHUNK)]
        for k in range(1, seq):
            both = both + stats[k][:, pl.ds(start, CHUNK)]
        both = jnp.transpose(jnp.concatenate([both, jnp.zeros((LANES - PAD, CHUNK), F32)], axis=0))
        scale = lax.rsqrt(both[:, 0:1] / inner + EPSILON)
        pull = scale * scale * scale * (both[:, 1:2] / inner)
        rows = pl.ds(start, CHUNK)
        gate, ssm, opened, silu = gate_terms(proj_ref, y_ref, rows, width)
        gated = ssm * silu
        grad_mixed = gm_ref[rows, :]
        plain = gated * scale
        mixed[rows, :] = (plain * gain).astype(BF16)
        grad_gated = scale * (grad_mixed * gain) - gated * pull
        gy_ref[rows, :] = (grad_gated * silu).astype(BF16)
        slope = opened * (1.0 + gate * (1.0 - opened))
        gg_ref[rows, :] = (grad_gated * ssm * slope).astype(BF16)
        return total + jnp.sum(grad_mixed * plain, axis=0, keepdims=True)

    gain_part_ref[0:1] = lax.fori_loop(0, length // CHUNK, chunk_step, jnp.zeros((1, width), F32))

    gate_w[...] = jnp.zeros_like(gate_w)
    out_w[...] = jnp.zeros_like(out_w)
    for k in range(seq):
        start = pl.multiple_of(lax.rem(s + k, seq) * rows_here, rows_here)
        rows = pl.ds(start, rows_here)
        gate_w[...] += mm_tn(normed_ref[rows, :], gg_ref[rows, :])
        out_w[...] += mm_tn(mixed[rows, :], cots[k][...])
    if packed:
        shard = model // (2 * line)
        piece = width // (2 * line)
        for p in range(line):
            for ref, parity in ((keep_ref, j), (send_ref, 1 - j)):
                at = 2 * p + parity
                ref[p, 0:shard, :] = gate_w[at_rows(at, shard), :].astype(ref.dtype)
                for c in range(model // width):
                    ref[p, shard + c * piece : shard + (c + 1) * piece, :] = out_w[
                        at_rows(at, piece), c * width : (c + 1) * width
                    ].astype(ref.dtype)


def backward_kernel(head_dim, dims, idx_ref, *refs):
    seq, line, first, final, packed = dims
    proj_ref, gy_ref, save_ref, xt_ref, bt_ref, heads_ref = refs[:6]
    refs = refs[6:]
    if not first:
        carried, refs = refs[:7], refs[7:]
    if final:
        gg_ref, weight_ref, normed_ref, gain_ref, gain_part_ref = refs[:5]
        gn_refs, refs = refs[5 : 5 + seq], refs[5 + seq :]
        if packed:
            keep_ref, send_ref, small_ref = refs[:3]
            refs = refs[3:]
        else:
            late_w, small_ref = refs[:2]
            refs = refs[2:]
        grad_ref, small_x_ref, small_b_ref, small_h_ref, dstate, next_x, next_b = refs[:7]
        refs = refs[7:]
        if packed:
            late_w, refs = refs[0], refs[1:]
        gn_scratch, xpad, bpad = refs
    else:
        grad_ref, small_x_ref, small_b_ref, small_h_ref, dstate, next_x, next_b = refs[:7]
        xpad, bpad = refs[7:]
    length, width = gy_ref.shape
    bc_width = bt_ref.shape[1]
    state_size = bc_width // 2
    head_count = width // head_dim
    per_tile = LANES // head_dim
    chunks = length // CHUNK
    half = chunks // 2
    dt_at = 2 * width + bc_width
    xpad[0:PAD] = jnp.zeros((PAD, width), F32)
    bpad[0:PAD] = jnp.zeros((PAD, bc_width), F32)
    low = 0 if final else half * CHUNK - PAD
    high = length if first else half * CHUNK
    xpad[PAD + low : PAD + high] = proj_ref[low:high, width : 2 * width].astype(F32)
    bpad[PAD + low : PAD + high] = proj_ref[low:high, 2 * width : dt_at].astype(F32)
    if first:
        for ref in (small_x_ref, small_b_ref, small_h_ref, dstate, next_x, next_b):
            ref[...] = jnp.zeros_like(ref)
    else:
        for ref, old in zip(
            (small_x_ref, small_b_ref, small_h_ref, dstate, next_x, next_b), carried[1:]
        ):
            ref[...] = old[...]
        grad_ref[half * CHUNK :, :] = carried[0][half * CHUNK :, :]
    row = iota((CHUNK, CHUNK), 0)
    col = iota((CHUNK, CHUNK), 1)
    causal = row >= col
    tril = causal.astype(F32)
    triu = (row <= col).astype(F32)
    strict = (row > col).astype(F32)
    lane = iota((CHUNK, LANES), 1)
    gather_heads = (
        iota((width, LANES), 0) // head_dim == iota((width, LANES), 1)
    ).astype(F32)

    def conv_back(grad_out, pre, padded_rows, taps, following, small_ref):
        gate = sigmoid(pre)
        grad_pre = grad_out * (gate * (1.0 + pre * (1.0 - gate)))
        extended = jnp.concatenate([grad_pre, following[...]], axis=0)
        following[...] = grad_pre[:PAD]
        total = jnp.zeros_like(grad_pre)
        sums = []
        for tap in range(4):
            total = total + taps[tap : tap + 1] * extended[3 - tap : 3 - tap + CHUNK]
            begin = PAD - 3 + tap
            sums.append(
                jnp.sum(grad_pre * padded_rows[begin : begin + CHUNK], axis=0, keepdims=True)
            )
        sums.append(jnp.sum(grad_pre, axis=0, keepdims=True))
        small_ref[0:5] = small_ref[0:5] + jnp.concatenate(sums, axis=0)
        return total

    def chunk_step(index, unused):
        chunk = (chunks if first else half) - 1 - index
        start = pl.multiple_of(chunk * CHUNK, CHUNK)
        x_rows = xpad[pl.ds(start, CHUNK + PAD), :]
        b_rows = bpad[pl.ds(start, CHUNK + PAD), :]
        u_x = conv_pre(x_rows, xt_ref[...])
        x = u_x * sigmoid(u_x)
        u_b = conv_pre(b_rows, bt_ref[...])
        bc = (u_b * sigmoid(u_b)).astype(BF16)
        b, c = bc[:, :state_size], bc[:, state_size:]
        raw, step, decay = decay_terms(
            proj_ref[pl.ds(start, CHUNK), dt_at:].astype(F32), heads_ref[...], tril
        )
        rate = heads_ref[1:2]
        decay_t = jnp.transpose(decay)
        step_t = jnp.transpose(step)
        scores = mm_nt(c, b)
        xb = x.astype(BF16)
        gy_b = gy_ref[pl.ds(start, CHUNK), :]
        gy = gy_b.astype(F32)
        old_b = save_ref[chunk]
        dnew = dstate[...]
        dnew_b = dnew.astype(BF16)
        last = decay[CHUNK - 1 : CHUNK]

        dscores = jnp.zeros((CHUNK, CHUNK), F32)
        row_sums = jnp.zeros((CHUNK, LANES), F32)
        col_sums = []
        within = []
        for tile in range(width // LANES):
            lanes = slice(tile * LANES, (tile + 1) * LANES)
            outer = mm_nt(gy_b[:, lanes], split_heads(xb[:, lanes], head_dim))
            mats = []
            for part in range(per_tile):
                head = tile * per_tile + part
                gap = decay[:, head : head + 1] - decay_t[head : head + 1, :]
                fade = jnp.exp(jnp.where(causal, gap, -1e30))
                plain = fade * scores
                mats.append(plain.astype(BF16))
                grad = outer[:, part * CHUNK : (part + 1) * CHUNK]
                scaled = grad * step_t[head : head + 1, :]
                dscores = dscores + scaled * fade
                col_sums.append(jnp.sum(grad * plain, axis=0, keepdims=True))
                rows = jnp.sum(scaled * plain, axis=1, keepdims=True)
                row_sums = row_sums + jnp.where(lane == head, rows, 0.0)
            within.append(
                mm_tn(jnp.concatenate(mats, axis=0), split_heads(gy_b[:, lanes], head_dim))
            )
        within = jnp.concatenate(within, axis=1)
        col_sums.append(jnp.zeros((LANES - head_count, CHUNK), F32))
        col_sums = jnp.transpose(jnp.concatenate(col_sums, axis=0))

        grown_gy = spread_heads(jnp.exp(decay), head_count, head_dim) * gy
        grown_gy_b = grown_gy.astype(BF16)
        remain = jnp.exp(last - decay)
        from_state = spread_heads(remain, head_count, head_dim) * mm_nn(b, dnew_b)
        carried_dot = mm_exact(grown_gy * mm_nn(c, old_b), gather_heads)
        state_dot = mm_exact(x * from_state, gather_heads)
        step_wide = spread_heads(step, head_count, head_dim)
        weight = spread_heads(remain * step, head_count, head_dim)
        dscores_b = dscores.astype(BF16)
        dc = mm_nn(dscores_b, b) + mm_nt(grown_gy_b, old_b)
        db = mm_tn(dscores_b, c) + mm_nt((weight * x).astype(BF16), dnew_b)
        last_wide = spread_heads(jnp.exp(last), head_count, head_dim)
        overlap = jnp.sum(old_b.astype(F32) * dnew, axis=0, keepdims=True) * last_wide
        dlast = mm_exact(jnp.broadcast_to(overlap, (PAD, width)), gather_heads)[0:1]
        dstate[...] = dnew * last_wide + mm_tn(c, grown_gy_b)

        direct = col_sums + state_dot
        ddecay = row_sums + carried_dot - step * col_sums
        da = mm_exact(triu, ddecay) + mm_exact(strict, step * state_dot) + dlast
        dstep = direct + da * rate
        ddt = dstep * sigmoid(raw)
        small_h_ref[0:1] = small_h_ref[0:1] + jnp.sum(ddt, axis=0, keepdims=True)
        small_h_ref[1:2] = small_h_ref[1:2] + jnp.sum(da * step, axis=0, keepdims=True) * rate

        dx = step_wide * (within + from_state) + xt_ref[5:6] * gy
        small_x_ref[5:6] = small_x_ref[5:6] + jnp.sum(gy * x, axis=0, keepdims=True)
        dx_in = conv_back(dx, u_x, x_rows, xt_ref[...], next_x, small_x_ref)
        dbc = jnp.concatenate([db, dc], axis=1)
        dbc_in = conv_back(dbc, u_b, b_rows, bt_ref[...], next_b, small_b_ref)
        grad_ref[pl.ds(start, CHUNK), :] = jnp.concatenate([dx_in, dbc_in, ddt], axis=1).astype(
            BF16
        )
        return unused

    lax.fori_loop(0, chunks - half if first else half, chunk_step, 0)
    if not final:
        return
    small_h_ref[2:3] = mm_exact(
        jnp.broadcast_to(small_x_ref[5:6], (PAD, width)), gather_heads
    )[0:1]
    s, j = idx_ref[0], idx_ref[2]
    model = normed_ref.shape[1]
    rows_here = gn_refs[0].shape[0]
    late_width = late_w.shape[1]
    gain_sum = jnp.zeros((1, model), F32)
    for k in range(seq):
        rows = pl.ds(pl.multiple_of(lax.rem(s + seq - k, seq) * rows_here, rows_here), rows_here)
        gn = mm_nt(gg_ref[rows, :], weight_ref[:, 0:width]) + mm_nt(
            grad_ref[rows, :], weight_ref[:, width:]
        )
        gn_refs[k][...] = gn.astype(gn_refs[k].dtype)
        gain_sum = gain_sum + jnp.sum(gn * normed_ref[rows, :].astype(F32), axis=0, keepdims=True)
        late = mm_tn(normed_ref[rows, :], grad_ref[rows, :])
        late_w[...] = late if k == 0 else late_w[...] + late
    gain_sum = gain_sum / gain_ref[...]
    small_ref[...] = jnp.zeros_like(small_ref)
    small_ref[0:5, 0:width] = small_x_ref[0:5]
    small_ref[0:5, width : width + bc_width] = small_b_ref[0:5]
    small_ref[0:3, width + bc_width :] = small_h_ref[0:3]
    small_ref[5:6, 0:width] = gain_part_ref[0:1]
    for c in range(0, model, late_width):
        size = min(late_width, model - c)
        at = 6 + c // late_width
        small_ref[at : at + 1, 0:size] = gain_sum[:, c : c + size]
    if packed:
        shard = model // (2 * line)
        for p in range(line):
            keep_ref[p] = late_w[at_rows(2 * p + j, shard), :]
            send_ref[p * shard : (p + 1) * shard, :] = late_w[
                at_rows(2 * p + 1 - j, shard), :
            ].astype(BF16)
        high = small_ref[...].astype(BF16)
        send_ref[line * shard : line * shard + PAD, :] = high
        send_ref[line * shard + PAD :, :] = (small_ref[...] - high.astype(F32)).astype(BF16)


def split_small(value):
    high = value.astype(BF16)
    return high, (value - high.astype(F32)).astype(BF16)


def join_small(ref, rows):
    return ref[rows : rows + PAD, :].astype(F32) + ref[rows + PAD : rows + 2 * PAD, :].astype(F32)


def pair_sum_kernel(dims, idx_ref, *refs):
    line, has_small = dims
    keep_ref, got_ref = refs[:2]
    refs = refs[2:]
    if has_small:
        small_ref, refs = refs[0], refs[1:]
    own_ref, refs = refs[0], refs[1:]
    if has_small:
        small_out, refs = refs[0], refs[1:]
    rows = own_ref.shape[0]
    p = idx_ref[1]
    if has_small:
        small = small_ref[...] + join_small(got_ref, line * rows)
        small_out[...] = small
        high, low = split_small(small)

    def block(at):
        return keep_ref[at] + got_ref[at_rows(at, rows), :].astype(F32)

    own_ref[...] = block(p)
    for k in range(1, line):
        ref = refs[k - 1]
        ref[0:rows] = block(lax.rem(p + line - k, line)).astype(BF16)
        if has_small:
            ref[rows : rows + PAD] = high
            ref[rows + PAD :] = low


def line_sum_kernel(dims, idx_ref, *refs):
    line, has_small = dims
    own_ref, refs = refs[0], refs[1:]
    if has_small:
        small_ref, refs = refs[0], refs[1:]
    got, outs = refs[: line - 1], refs[line - 1 :]
    rows = own_ref.shape[0]
    total = own_ref[...]
    for ref in got:
        total = total + ref[0:rows].astype(F32)
    if has_small:
        out_ref = outs[0]
        small = small_ref[...]
        for ref in got:
            small = small + join_small(ref, rows)
        out_ref[0:rows] = total.astype(BF16)
        high, low = split_small(small)
        out_ref[rows : rows + PAD] = high
        out_ref[rows + PAD :] = low
    else:
        at = outs[0].shape[0]
        outs[0][...] = total[:at].astype(BF16)
        outs[1][...] = total[at:].astype(BF16)


def finish_kernel(dims, idx_ref, *refs):
    seq, shard, width, bc_width, heads_here = dims
    gates, refs = refs[:seq], refs[seq:]
    outs, refs = refs[:seq], refs[seq:]
    lates, refs = refs[:seq], refs[seq:]
    in_ref, dt_ref, out_ref, gain_ref, cx_ref, cxb_ref, cbc_ref, cbcb_ref = refs[:8]
    bias_ref, rate_ref, skip_ref, gate_ref = refs[8:12]
    wide_x, heads_sum = refs[12:]
    inner = seq * width
    model = out_ref.shape[1]
    s = idx_ref[0]
    head_at = width + bc_width
    piece = outs[0].shape[0] // (model // width)
    bc_sum = jnp.zeros((shard, bc_width), F32)
    dt_sum = jnp.zeros((shard, LANES), F32)
    bc_small = jnp.zeros((PAD, bc_width), F32)
    head_small = jnp.zeros((PAD, LANES), F32)
    gain_sum = jnp.zeros((2, lates[0].shape[1]), F32)
    for k in range(seq):
        owner = lax.rem(s + k, seq)
        cols = pl.ds(pl.multiple_of(owner * width, LANES), width)
        in_ref[:, cols] = gates[k][...].astype(F32)
        cols_x = pl.ds(pl.multiple_of(inner + owner * width, LANES), width)
        in_ref[:, cols_x] = lates[k][0:shard, 0:width].astype(F32)
        bc_sum = bc_sum + lates[k][0:shard, width:head_at].astype(F32)
        dt_sum = dt_sum + pltpu.roll(
            lates[k][0:shard, head_at:].astype(F32), owner * heads_here, axis=1
        )
        sub = lax.rem(s + seq - k, seq)
        for c in range(model // width):
            out_ref[at_rows(sub, piece), c * width : (c + 1) * width] = outs[k][
                c * piece : (c + 1) * piece
            ].astype(F32)
        small = join_small(lates[k], shard)
        wide_x[:, cols] = small[:, 0:width]
        bc_small = bc_small + small[:, width:head_at]
        head_small = head_small + pltpu.roll(small[:, head_at:], owner * heads_here, axis=1)
        gain_sum = gain_sum + small[6:8]
    in_ref[:, 2 * inner :] = bc_sum
    dt_ref[...] = dt_sum[:, 0 : dt_ref.shape[1]]
    cx_ref[...] = wide_x[0:4]
    cxb_ref[...] = wide_x[4:5]
    gate_ref[...] = wide_x[5:6]
    cbc_ref[...] = bc_small[0:4]
    cbcb_ref[...] = bc_small[4:5]
    all_heads = bias_ref.shape[1]
    bias_ref[...] = head_small[0:1, 0:all_heads]
    rate_ref[...] = head_small[1:2, 0:all_heads]
    skip_ref[...] = head_small[2:3, 0:all_heads]
    width_late = gain_sum.shape[1]
    for c in range(0, model, width_late):
        size = min(width_late, model - c)
        at = c // width_late
        gain_ref[:, c : c + size] = gain_sum[at : at + 1, 0:size]


VMEM_SPEC = pl.BlockSpec(memory_space=pltpu.VMEM)
SMEM_SPEC = pl.BlockSpec(memory_space=pltpu.SMEM)


def call(kernel, name, idx, arrays, outs, scratch, flops):
    bytes_moved = sum(a.size * a.dtype.itemsize for a in list(arrays) + list(outs))
    return pl.pallas_call(
        kernel,
        out_shape=tuple(outs),
        in_specs=[SMEM_SPEC] + [VMEM_SPEC] * len(arrays),
        out_specs=tuple([VMEM_SPEC] * len(outs)),
        scratch_shapes=[pltpu.VMEM(*one) for one in scratch],
        compiler_params=pltpu.CompilerParams(vmem_limit_bytes=VMEM_LIMIT),
        cost_estimate=pl.CostEstimate(
            flops=int(flops), bytes_accessed=int(bytes_moved), transcendentals=0
        ),
        name=name,
    )(idx, *arrays)


def shaped(shape, dtype):
    return jax.ShapeDtypeStruct(shape, dtype)


def put(buffer, value, index, axis=0):
    return lax.dynamic_update_index_in_dim(buffer, value, index, axis)


def take(array, index, axis=0):
    return lax.dynamic_index_in_dim(array, index, axis, keepdims=False)


class Ring:
    def __init__(self):
        self.seq = lax.axis_size("seq")
        self.fsdp = lax.axis_size("fsdp")
        self.line = self.fsdp // 2
        self.s = lax.axis_index("seq")
        f = lax.axis_index("fsdp")
        self.p, self.j = f // 2, f % 2

    def from_seq(self, value, k):
        n = self.seq
        return lax.ppermute(value, "seq", [((i + k) % n, i) for i in range(n)])

    def from_line(self, value, k):
        n = self.line
        pairs = [(((i + k) % n) * 2 + c, i * 2 + c) for i in range(n) for c in range(2)]
        return lax.ppermute(value, "fsdp", pairs)

    def from_sibling(self, value):
        return lax.ppermute(value, "fsdp", [(i ^ 1, i) for i in range(self.fsdp)])

    def parts_seq(self, value):
        return [value] + [self.from_seq(value, k) for k in range(1, self.seq)]

    def parts_line(self, value):
        return [value] + [self.from_line(value, k) for k in range(1, self.line)]

    def gather_seq(self, value):
        whole = jnp.zeros((self.seq,) + value.shape, value.dtype)
        for k in range(self.seq):
            part = value if k == 0 else self.from_seq(value, k)
            whole = put(whole, part, (self.s + k) % self.seq)
        return whole

    def gather_line(self, value):
        whole = jnp.zeros((self.line,) + value.shape, value.dtype)
        for k in range(self.line):
            part = value if k == 0 else self.from_line(value, k)
            whole = put(whole, part, (self.p + k) % self.line)
        return whole

    def join_sibling(self, mine):
        other = self.from_sibling(mine)
        whole = jnp.zeros((mine.shape[0], 2) + mine.shape[1:], mine.dtype)
        whole = put(whole, mine, self.j, 1)
        return put(whole, other, 1 - self.j, 1)

    def sum_seq(self, blocks):
        total = take(blocks, self.s).astype(F32)
        for k in range(1, self.seq):
            total = total + self.from_seq(
                take(blocks, (self.s - k) % self.seq), k
            ).astype(F32)
        return total

    def pair_split(self, blocks, extra=None):
        pairs = blocks.reshape((self.line, 2) + blocks.shape[1:])
        keep = take(pairs, self.j, 1)
        send = take(pairs, 1 - self.j, 1).astype(BF16)
        if extra is None:
            return keep, send
        send = send.reshape((-1, send.shape[2]))
        return keep, jnp.concatenate([send, halves(extra)], axis=0)

    def sum_fsdp(self, keep, send, extra=None):
        got = self.from_sibling(send)
        if extra is None:
            mine = keep + got.astype(F32)
        else:
            rows = keep.shape[0] * keep.shape[1]
            mine = keep + got[:rows].reshape(keep.shape).astype(F32)
            extra = extra + whole_of(got[rows:])
        total = take(mine, self.p)
        extra_total = extra
        for k in range(1, self.line):
            sent = take(mine, (self.p - k) % self.line).astype(BF16)
            if extra is None:
                total = total + self.from_line(sent, k).astype(F32)
            else:
                rows = sent.shape[0]
                got = self.from_line(jnp.concatenate([sent, halves(extra)], axis=0), k)
                total = total + got[:rows].astype(F32)
                extra_total = extra_total + whole_of(got[rows:])
        return total, extra_total


def halves(value):
    high = lax.reduce_precision(value, 8, 7)
    return jnp.concatenate([high.astype(BF16), (value - high).astype(BF16)], axis=0)


def whole_of(pair):
    rows = pair.shape[0] // 2
    return pair[:rows].astype(F32) + pair[rows:].astype(F32)


def local(
    tokens,
    norm_gain,
    in_weight,
    dt_weight,
    conv_x_weight,
    conv_x_bias,
    conv_bc_weight,
    conv_bc_bias,
    dt_bias,
    a_log,
    d_skip,
    gate_gain,
    out_weight,
    cotangent,
):
    ring = Ring()
    s, seq, fsdp, line = ring.s, ring.seq, ring.fsdp, ring.line
    idx = jnp.stack([ring.s, ring.p, ring.j]).astype(jnp.int32)
    tok_rows, cot_rows = tokens[0], cotangent[0]
    rows_here, model = tok_rows.shape
    length = rows_here * seq
    inner = gate_gain.shape[0]
    width = inner // seq
    all_heads = dt_bias.shape[0]
    head_dim = inner // all_heads
    heads_here = all_heads // seq
    bc_width = conv_bc_weight.shape[1]
    state_size = bc_width // 2
    shard = in_weight.shape[0]
    wide = -(-width // LANES) * LANES
    late_width = wide + bc_width + LANES
    chunks = length // CHUNK
    packed = wide == width and shard % 16 == 0 and (width // fsdp) % 16 == 0 and model % width == 0

    def columns(array, start, size):
        return lax.dynamic_slice_in_dim(array, start, size, 1)

    def pad_lanes(array, value=0.0, size=LANES):
        return jnp.pad(array, ((0, 0), (0, size - array.shape[1])), constant_values=value)

    own_weight = jnp.concatenate(
        [
            pad_lanes(columns(in_weight, s * width, width), size=wide),
            pad_lanes(columns(in_weight, inner + s * width, width), size=wide),
            in_weight[:, 2 * inner :],
            pad_lanes(columns(dt_weight, s * heads_here, heads_here)),
        ],
        axis=1,
    )
    x_taps = columns(
        jnp.concatenate(
            [
                conv_x_weight,
                conv_x_bias[None],
                jnp.repeat(d_skip, head_dim)[None],
                gate_gain[None],
                jnp.zeros((1, inner), F32),
            ],
            axis=0,
        ),
        s * width,
        width,
    )
    x_taps = pad_lanes(x_taps, size=wide)
    bc_taps = jnp.concatenate(
        [conv_bc_weight, conv_bc_bias[None], jnp.zeros((3, bc_width), F32)], axis=0
    )
    bias_here = columns(dt_bias[None], s * heads_here, heads_here)
    rate_here = -jnp.exp(columns(a_log[None], s * heads_here, heads_here))
    heads = jnp.concatenate(
        [pad_lanes(bias_here, -100.0), pad_lanes(rate_here), jnp.zeros((6, LANES), F32)], axis=0
    )
    gain_row = norm_gain[None]

    tok_parts = ring.parts_seq(tok_rows)
    if packed:
        lane_parts = ring.parts_line(own_weight)
        lane_parts, idx, gain_row, x_taps, bc_taps, heads = lax.optimization_barrier(
            (lane_parts, idx, gain_row, x_taps, bc_taps, heads)
        )
        pieces = lane_parts + [ring.from_sibling(part) for part in lane_parts]
    else:
        pieces = [ring.join_sibling(ring.gather_line(own_weight)).reshape(model, -1)]
    tok_parts, pieces, cot_rows, out_weight = lax.optimization_barrier(
        (tok_parts, pieces, cot_rows, out_weight)
    )
    cot_parts = ring.parts_seq(cot_rows)
    out_rows = line // seq
    out_got = []
    for r in range(out_rows):
        place = s * out_rows + r
        got = [jnp.where(ring.p == place, out_weight, jnp.zeros_like(out_weight))]
        for k in range(1, line):
            pairs = []
            for one in range(seq):
                src = one * out_rows + r
                dst = (src + k) % line
                for c in range(2):
                    pairs.append((one * fsdp + 2 * src + c, one * fsdp + 2 * dst + c))
            got.append(lax.ppermute(out_weight, ("seq", "fsdp"), pairs))
        out_got.append(got)
    pads = [((length + PAD, wide), F32), ((length + PAD, bc_width), F32)]
    projected, ssm_out, saved, weight, normed = call(
        functools.partial(forward_kernel, head_dim, (seq, line, len(pieces))),
        "project_scan",
        idx,
        tok_parts + pieces + [gain_row, x_taps, bc_taps, heads],
        [
            shaped((length, wide + late_width), BF16),
            shaped((length, wide), BF16),
            shaped((chunks, state_size, wide), BF16),
            shaped((model, wide + late_width), BF16),
            shaped((length, model), BF16),
        ],
        pads + [((state_size, wide), F32)],
        8 * length * wide * CHUNK,
    )
    out_got, ssm_out, projected = lax.optimization_barrier((out_got, ssm_out, projected))
    out_mine = [sum(got[1:], got[0]) for got in out_got]
    out_here = ring.join_sibling(jnp.stack(out_mine)).reshape(width, model)
    out_here = jnp.pad(out_here, ((0, wide - width), (0, 0)))
    grad_mixed, stats = call(
        functools.partial(stats_kernel, seq),
        "gate_stats",
        idx,
        cot_parts + [out_here, projected, ssm_out, x_taps],
        [shaped((length, wide), F32), shaped((PAD, length), F32)],
        [],
        2 * length * wide * model,
    )
    stat_parts = ring.parts_seq(stats)
    out_parts = call(
        functools.partial(result_kernel, seq),
        "out_project",
        idx,
        [projected, ssm_out, x_taps, out_here],
        [shaped((rows_here, model), F32 if k == 0 else BF16) for k in range(seq)],
        [],
        2 * length * wide * model,
    )
    out_parts, stat_parts = lax.optimization_barrier((out_parts, stat_parts))
    out_got = [out_parts[0]] + [ring.from_seq(out_parts[k], k) for k in range(1, seq)]

    extra_rows = (width // fsdp) * (model // width)
    grid_w = ((model, wide), F32), ((wide, model), F32), ((length, wide), BF16)
    if packed:
        outs = [
            shaped((line, shard + extra_rows, width), F32),
            shaped((line, shard + extra_rows, width), BF16),
        ]
        scratch = [grid_w[2], grid_w[0], grid_w[1]]
    else:
        outs = [shaped(*grid_w[0]), shaped(*grid_w[1])]
        scratch = [grid_w[2]]
    grad_ssm, grad_gate, gain_part, one, two = call(
        functools.partial(gate_kernel, (seq, line, inner, packed)),
        "gate_backward",
        idx,
        cot_parts + stat_parts + [projected, ssm_out, grad_mixed, x_taps, normed],
        [
            shaped((length, wide), BF16),
            shaped((length, wide), BF16),
            shaped((PAD, wide), F32),
        ]
        + outs,
        scratch,
        4 * length * wide * model,
    )
    if packed:
        keep, send = one, two
    else:
        out_blocks = two[:width].reshape(fsdp, width // fsdp, model)
        keep, send = ring.pair_split(
            jnp.concatenate(
                [one[:, :width].reshape(fsdp, shard, width)]
                + [out_blocks[:, :, c : c + width] for c in range(0, model, width)],
                axis=1,
            )
        )
    base = [projected, grad_ssm, saved, x_taps, bc_taps, heads]
    state_outs = [
        shaped((length, late_width), BF16),
        shaped((PAD, wide), F32),
        shaped((PAD, bc_width), F32),
        shaped((PAD, LANES), F32),
        shaped((state_size, wide), F32),
        shaped((PAD, wide), F32),
        shaped((PAD, bc_width), F32),
    ]
    carried = call(
        functools.partial(backward_kernel, head_dim, (seq, line, True, False, packed)),
        "scan_back_late",
        idx,
        base,
        state_outs,
        pads,
        12 * length * wide * CHUNK,
    )
    out_got, carried = lax.optimization_barrier((out_got, carried))
    if packed:
        early_rows = shard + extra_rows
        got = ring.from_sibling(send)
        got, carried = lax.optimization_barrier((got, carried))
        early_own, *sends = call(
            functools.partial(pair_sum_kernel, (line, False)),
            "pair_sum_early",
            idx,
            [keep, got.reshape(line * early_rows, width)],
            [shaped((early_rows, width), F32)]
            + [shaped((early_rows, width), BF16)] * (line - 1),
            [],
            0,
        )
        sends, carried = lax.optimization_barrier((sends, carried))
        early_got = [ring.from_line(sends[k - 1], k) for k in range(1, line)]
    small_shape = ((PAD, late_width), F32)
    late_shape = ((model, late_width), F32)
    if packed:
        outs = [
            shaped((line, shard, late_width), F32),
            shaped((line * shard + 2 * PAD, late_width), BF16),
            shaped(*small_shape),
        ]
        scratch = [(o.shape, o.dtype) for o in state_outs] + [late_shape]
    else:
        outs = [shaped(*late_shape), shaped(*small_shape)]
        scratch = [(o.shape, o.dtype) for o in state_outs]
    done = call(
        functools.partial(backward_kernel, head_dim, (seq, line, False, True, packed)),
        "scan_back_early",
        idx,
        base + list(carried) + [grad_gate, weight, normed, gain_row, gain_part],
        [shaped((rows_here, model), F32 if k == 0 else BF16) for k in range(seq)] + outs,
        scratch + [((PAD, LANES), F32)] + pads,
        12 * length * wide * CHUNK + 4 * length * model * late_width,
    )
    gn_parts, done = done[:seq], done[seq:]
    if packed:
        keep, send, small = done
        early_got, gn_parts, send = lax.optimization_barrier((early_got, gn_parts, send))
        got = ring.from_sibling(send)
        gn_got = [ring.from_seq(gn_parts[k], k) for k in range(1, seq)]
        gate_own, out_own = call(
            functools.partial(line_sum_kernel, (line, False)),
            "line_sum_early",
            idx,
            [early_own] + early_got,
            [shaped((shard, width), BF16), shaped((extra_rows, width), BF16)],
            [],
            0,
        )
        got, gate_own, out_own = lax.optimization_barrier((got, gate_own, out_own))
        late_own, small_sum, *sends = call(
            functools.partial(pair_sum_kernel, (line, True)),
            "pair_sum_late",
            idx,
            [keep, got, small],
            [shaped((shard, late_width), F32), shaped(*small_shape)]
            + [shaped((shard + 2 * PAD, late_width), BF16)] * (line - 1),
            [],
            0,
        )
        sends, gate_own, out_own = lax.optimization_barrier((sends, gate_own, out_own))
        late_got = [ring.from_line(sends[k - 1], k) for k in range(1, line)]
        gate_got = ring.parts_seq(gate_own)
        block_got = []
        for k in range(seq):
            pairs = []
            for one in range(seq * fsdp):
                pairs.append((one, ((one + k) % seq) * fsdp + one // seq))
            block_got.append(lax.ppermute(out_own, ("seq", "fsdp"), pairs))
        (late_all,) = call(
            functools.partial(line_sum_kernel, (line, True)),
            "line_sum_late",
            idx,
            [late_own, small_sum] + late_got,
            [shaped((shard + 2 * PAD, late_width), BF16)],
            [],
            0,
        )
        late_all, gn_got, gate_got, block_got = lax.optimization_barrier(
            (late_all, gn_got, gate_got, block_got)
        )
        lates = ring.parts_seq(late_all)
        finals = call(
            functools.partial(finish_kernel, (seq, shard, width, bc_width, heads_here)),
            "finish",
            idx,
            gate_got + block_got + lates,
            [
                shaped((shard, in_weight.shape[1]), F32),
                shaped((shard, all_heads), F32),
                shaped(out_weight.shape, F32),
                shaped((1, model), F32),
                shaped((4, inner), F32),
                shaped((1, inner), F32),
                shaped((4, bc_width), F32),
                shaped((1, bc_width), F32),
                shaped((1, all_heads), F32),
                shaped((1, all_heads), F32),
                shaped((1, all_heads), F32),
                shaped((1, inner), F32),
            ],
            [((PAD, inner), F32), ((PAD, LANES), F32)],
            0,
        )
        (
            in_weight_grad,
            dt_weight_grad,
            out_weight_grad,
            norm_gain_grad,
            conv_x_grad,
            conv_x_bias_grad,
            conv_bc_grad,
            conv_bc_bias_grad,
            dt_bias_grad,
            a_log_grad,
            d_skip_grad,
            gate_gain_grad,
        ) = finals
        norm_gain_grad, conv_x_bias_grad, conv_bc_bias_grad, gate_gain_grad = (
            norm_gain_grad.reshape(-1),
            conv_x_bias_grad.reshape(-1),
            conv_bc_bias_grad.reshape(-1),
            gate_gain_grad.reshape(-1),
        )
        dt_bias_grad, a_log_grad, d_skip_grad = (
            dt_bias_grad.reshape(-1),
            a_log_grad.reshape(-1),
            d_skip_grad.reshape(-1),
        )
    else:
        early, unused = ring.sum_fsdp(keep, send)
        out_block = lax.ppermute(
            early[shard:].astype(BF16),
            ("seq", "fsdp"),
            [(k, (k % seq) * fsdp + k // seq) for k in range(seq * fsdp)],
        )
        early = ring.gather_seq(jnp.concatenate([early[:shard].astype(BF16), out_block], axis=0))
        gate_weight_grad = early[:, :shard]
        out_weight_grad = early[:, shard:].reshape(seq, model // width, width // fsdp, width)
        out_weight_grad = out_weight_grad.transpose(0, 2, 1, 3).reshape(-1, model).astype(F32)

        gn_got = [ring.from_seq(gn_parts[k], k) for k in range(1, seq)]
        late_part, small = done
        keep, send = ring.pair_split(late_part.reshape(fsdp, shard, late_width), small)
        late, small = ring.sum_fsdp(keep, send, small)
        late = ring.gather_seq(jnp.concatenate([late.astype(BF16), halves(small)], axis=0))
        small = late[:, shard : shard + PAD].astype(F32) + late[:, shard + PAD :].astype(F32)
        head_at = wide + bc_width
        conv_x = small[:, :5, :width].transpose(1, 0, 2).reshape(5, inner)
        conv_bc = small[:, :5, wide:head_at].sum(0)
        head_grads = small[:, :3, head_at : head_at + heads_here].transpose(1, 0, 2)
        head_grads = head_grads.reshape(3, all_heads)
        gate_gain_grad = small[:, 5, :width].reshape(-1)
        norm_gain_grad = small[:, 6:].sum(0).reshape(-1)[:model]

        late = late[:, :shard].astype(F32)
        in_weight_grad = jnp.concatenate(
            [
                gate_weight_grad.astype(F32).transpose(1, 0, 2).reshape(shard, inner),
                late[:, :, :width].transpose(1, 0, 2).reshape(shard, inner),
                late[:, :, wide:head_at].sum(0),
            ],
            axis=1,
        )
        dt_weight_grad = late[:, :, head_at : head_at + heads_here].transpose(1, 0, 2)
        dt_weight_grad = dt_weight_grad.reshape(shard, all_heads)
        conv_x_grad, conv_x_bias_grad = conv_x[:4], conv_x[4]
        conv_bc_grad, conv_bc_bias_grad = conv_bc[:4], conv_bc[4]
        dt_bias_grad, a_log_grad, d_skip_grad = head_grads[0], head_grads[1], head_grads[2]

    out_sum = out_got[0]
    grad_normed = gn_parts[0]
    for k in range(1, seq):
        out_sum = out_sum + out_got[k].astype(F32)
        grad_normed = grad_normed + gn_got[k - 1].astype(F32)
    stats_here = lax.dynamic_slice_in_dim(sum(stat_parts)[0], s * rows_here, rows_here, 0)
    out_scale = lax.rsqrt(stats_here / inner + EPSILON)[:, None]
    result = tok_rows.astype(F32) + out_sum * out_scale

    tok_wide = tok_rows.astype(F32)
    scale = lax.rsqrt(jnp.mean(tok_wide * tok_wide, axis=-1, keepdims=True) + EPSILON)
    gained = grad_normed * norm_gain
    grad_tok = scale * gained - tok_wide * (
        scale * scale * scale * jnp.mean(gained * tok_wide, axis=-1, keepdims=True)
    )
    grad_tokens = cot_rows.astype(F32) + grad_tok
    return (
        result[None],
        grad_tokens[None],
        norm_gain_grad,
        in_weight_grad,
        dt_weight_grad,
        conv_x_grad,
        conv_x_bias_grad,
        conv_bc_grad,
        conv_bc_bias_grad,
        dt_bias_grad,
        a_log_grad,
        d_skip_grad,
        gate_gain_grad,
        out_weight_grad,
    )


def solution(mesh):
    placed = (
        P("fsdp", "seq", None),
        P(),
        P("fsdp", None),
        P("fsdp", None),
        P(),
        P(),
        P(),
        P(),
        P(),
        P(),
        P(),
        P(),
        P("fsdp", None),
        P("fsdp", "seq", None),
    )
    return jax.shard_map(
        local,
        mesh=mesh,
        in_specs=placed,
        out_specs=(
            P("fsdp", "seq", None),
            P("fsdp", "seq", None),
            P(),
            P("fsdp", None),
            P("fsdp", None),
            P(),
            P(),
            P(),
            P(),
            P(),
            P(),
            P(),
            P(),
            P("fsdp", None),
        ),
        check_vma=False,
    )
```
